32 devices in a mesh: frow: 8 (over z, y), fcol: 4 (over x, core).
Axes of the slice: x: 2, y: 2, z: 4, core: 2. Of those that a mesh axis runs over, the one named last changes fastest.
Arguments:
- image: bfloat16 [2, 4096, 2048], P(None, 'frow', 'fcol'), may hold values from -6 to 6
- window_rows: float32 [4096], P('frow'), may hold values from 0.1 to 1.9
- window_cols: float32 [2048], P('fcol'), may hold values from 0.1 to 1.9
- w_terms: float32 [2], replicated, may hold values from 20 to 200
- facet_row_offset: int32 [8], replicated, may hold values from 0 to 65535
- facet_col_offset: int32 [4], replicated, may hold values from 0 to 65535
- band_offset: int32 [2], replicated, may hold values from 0 to 65535
- sub_row_offset: int32 [2], replicated, may hold values from 0 to 65535
- sub_column: int32 [2], replicated, may hold values from 0 to 1, as said below
Outputs:
- subgrids: float32 [2, 2, 512, 512], P(None, None, 'frow', 'fcol')
The draws below stay inside these ranges and needn't reach their ends.
Inputs may be any that keep to these rules, and one draw needn't show every extreme that they name: `sub_column`: every subgrid column holds exactly 1 subgrids.
All inputs are finite; a program needn't handle non-finite values.
Results may differ from the reference program's by a relative error of at most 0.0052.
Values sent between devices are 32-bit elements; how exact they have to be, the bound alone decides.
A program may use at most 64 MiB of HBM per device.

```python
import math
import jax
import jax.numpy as jnp
from jax import lax

F = 512
SG = 512
IMAGE = 65536
COLS = 2
SUB = 2
NX = 4096
NY = 2048
N_FROW = 8
N_FCOL = 4


def draw_sub_column(key, part):
    order = jax.random.permutation(jax.random.fold_in(key, 17), SUB)
    return (order % COLS).astype(jnp.int32)


def plant(result, stream_key, low, high):
    longest = result.shape.index(max(result.shape))
    spots = []
    for shift in (0, 1):
        where = [jax.random.randint(jax.random.fold_in(stream_key, axis), (), 0, length) for axis, length in enumerate(result.shape)]
        where[longest] = (where[longest] + shift) % result.shape[longest]
        spots.append(tuple(where))
    return result.at[spots[0]].set(low).at[spots[1]].set(high)


def level_of(stream_key, shape, shards, low, high):
    def one(axis_at, blocks):
        draws = jax.random.uniform(jax.random.fold_in(jax.random.fold_in(stream_key, 6), axis_at), (blocks,), jnp.float32, low / len(shards), high / len(shards))
        return jnp.repeat(jnp.exp(draws), shape[axis_at] // blocks).reshape((-1,) + (1,) * (len(shape) - axis_at - 1))

    gain = one(*shards[0])
    for cut in shards[1:]:
        gain = gain * one(*cut)
    return gain


def gaussian(key, shape, width, limit, split=(), kind=jnp.bfloat16):
    level = level_of(key, shape, split, -0.22, 0.18) if split else 1.0
    result = jax.random.normal(key, shape, jnp.float32) * width * level
    return jnp.minimum(jnp.maximum(result, -limit), limit).astype(kind)


def setup_inputs(seed: int = 0) -> dict:
    arg_keys = jax.random.split(jax.random.key(seed), 10)
    return {
        "image": gaussian(arg_keys[0], (2, NX, NY), 1.0, 6.0, ((1, 8), (2, 4))),
        "window_rows": jnp.clip(1.0 + 0.18 * jax.random.normal(arg_keys[1], (NX,), jnp.float32), 0.1, 1.9),
        "window_cols": jnp.clip(1.0 + 0.18 * jax.random.normal(arg_keys[2], (NY,), jnp.float32), 0.1, 1.9),
        "w_terms": jnp.clip(jax.random.uniform(arg_keys[3], (COLS,), jnp.float32, 20.0, 200.0), 20.0, 200.0),
        "facet_row_offset": plant(jax.random.randint(arg_keys[4], (N_FROW,), 0, IMAGE), jax.random.fold_in(arg_keys[4], 1), 0, IMAGE - 1).astype(jnp.int32),
        "facet_col_offset": plant(jax.random.randint(arg_keys[5], (N_FCOL,), 0, IMAGE), jax.random.fold_in(arg_keys[5], 1), 0, IMAGE - 1).astype(jnp.int32),
        "band_offset": jax.random.randint(arg_keys[6], (COLS,), 0, IMAGE).astype(jnp.int32),
        "sub_row_offset": jax.random.randint(arg_keys[7], (SUB,), 0, IMAGE).astype(jnp.int32),
        "sub_column": draw_sub_column(jax.random.fold_in(arg_keys[9], 71), 0),
    }


def phase_index(first, second):
    high = first * (second // 256) % 256 * 256
    return (high + first * (second % 256)) % 65536

def dft_table(coords, freqs):
    angle = phase_index(coords, freqs).astype(jnp.float32) * (2.0 * math.pi / IMAGE)
    return (jnp.cos(angle).astype(jnp.bfloat16), (-jnp.sin(angle)).astype(jnp.bfloat16))

def coord_unit(coords):
    return (coords % IMAGE).astype(jnp.float32) / IMAGE - 0.5

def prepare(real_part, imag_part, wrow, wcol, grow, gcol, w_value):
    lcoord = coord_unit(grow)
    mcoord = coord_unit(gcol)
    angle = w_value * (lcoord[:, None] ** 2 + mcoord[None, :] ** 2)
    scale = wrow[:, None] * wcol[None, :]
    first = real_part.astype(jnp.float32) * scale
    second = imag_part.astype(jnp.float32) * scale
    cosine = jnp.cos(angle)
    sine = jnp.sin(angle)
    return ((first * cosine - second * sine).astype(jnp.bfloat16), (first * sine + second * cosine).astype(jnp.bfloat16))

def matmul(left, right):
    return jnp.dot(left.astype(jnp.float32), right.astype(jnp.float32), precision=lax.Precision.HIGHEST)

def reference(image, window_rows, window_cols, w_terms, facet_row_offset, facet_col_offset, band_offset, sub_row_offset, sub_column):
    local = jnp.arange(F, dtype=jnp.int32)
    freq_base = jnp.arange(SG, dtype=jnp.int32)

    def row_step(total, row_index):
        wrow = lax.dynamic_slice(window_rows, ((row_index * F).astype(jnp.int32),), (F,))
        grow = facet_row_offset[row_index] + local

        def col_step(acc, col_index):
            pixels = lax.dynamic_slice(image, (jnp.int32(0), (row_index * F).astype(jnp.int32), (col_index * F).astype(jnp.int32)), (2, F, F))
            wcol = lax.dynamic_slice(window_cols, ((col_index * F).astype(jnp.int32),), (F,))
            gcol = facet_col_offset[col_index] + local
            pieces = []
            for column in range(COLS):
                prep_re, prep_im = prepare(pixels[0], pixels[1], wrow, wcol, grow, gcol, w_terms[column])
                table_re, table_im = dft_table(gcol[:, None], band_offset[column] + freq_base[None, :])
                out_re = matmul(prep_re, table_re) - matmul(prep_im, table_im)
                out_im = matmul(prep_re, table_im) + matmul(prep_im, table_re)
                pieces.append(jnp.stack([out_re, out_im], axis=1))
            return (acc + jnp.stack(pieces, axis=1), None)
        summed, _ = lax.scan(col_step, jnp.zeros((F, COLS, 2, SG), jnp.float32), jnp.arange(N_FCOL, dtype=jnp.int32))
        banded = (summed / math.sqrt(NY)).astype(jnp.bfloat16)
        results = []
        for sub_index in range(SUB):
            table_re, table_im = dft_table(grow[:, None], sub_row_offset[sub_index] + freq_base[None, :])
            chosen = banded[:, sub_column[sub_index]]
            band_re = chosen[:, 0]
            band_im = chosen[:, 1]
            out_re = matmul(table_re.T, band_re) - matmul(table_im.T, band_im)
            out_im = matmul(table_re.T, band_im) + matmul(table_im.T, band_re)
            results.append(jnp.stack([out_re, out_im], axis=0))
        return (total + jnp.stack(results, axis=0) / math.sqrt(NX), None)
    subgrids, _ = lax.scan(row_step, jnp.zeros((SUB, 2, SG, SG), jnp.float32), jnp.arange(N_FROW, dtype=jnp.int32))
    return subgrids
```

```python
import functools
import math

import jax
import jax.numpy as jnp
from jax import lax
from jax.experimental import pallas as pl
from jax.experimental.pallas import tpu as pltpu
from jax.sharding import PartitionSpec as P

SG = 512
IMAGE = 65536


def phase_index(first, second):
    high = first * (second // 256) % 256 * 256
    return (high + first * (second % 256)) % 65536


def dft_table(coords, freqs):
    angle = phase_index(coords, freqs).astype(jnp.float32) * (2.0 * math.pi / IMAGE)
    return (jnp.cos(angle).astype(jnp.bfloat16), (-jnp.sin(angle)).astype(jnp.bfloat16))


def coord_unit(coords):
    return (coords % IMAGE).astype(jnp.float32) / IMAGE - 0.5


def block_table(table_re, table_im):
    upper = jnp.concatenate([table_re, table_im], axis=1)
    lower = jnp.concatenate([-table_im, table_re], axis=1)
    return jnp.concatenate([upper, lower], axis=0)


def general_local(
    image,
    window_rows,
    window_cols,
    w_terms,
    facet_row_offset,
    facet_col_offset,
    band_offset,
    sub_row_offset,
    sub_column,
):
    facet = image.shape[1]
    column_count = band_offset.shape[0]
    sub_count = sub_row_offset.shape[0]
    frow_index = lax.axis_index("frow")
    fcol_index = lax.axis_index("fcol")
    freq_base = jnp.arange(SG, dtype=jnp.int32)
    gcol = facet_col_offset[fcol_index] + jnp.arange(image.shape[2], dtype=jnp.int32)
    mcoord = coord_unit(gcol)
    row_base = facet_row_offset[frow_index]
    row_ids = row_base + jnp.arange(facet, dtype=jnp.int32)
    radius = coord_unit(row_ids)[:, None] ** 2 + mcoord[None, :] ** 2
    scale = window_rows[:, None] * window_cols[None, :]
    first = image[0].astype(jnp.float32) * scale
    second = image[1].astype(jnp.float32) * scale
    prepared = []
    for column in range(column_count):
        angle = w_terms[column] * radius
        cosine = jnp.cos(angle)
        sine = jnp.sin(angle)
        prep_re = (first * cosine - second * sine).astype(jnp.bfloat16)
        prep_im = (first * sine + second * cosine).astype(jnp.bfloat16)
        prepared.append(jnp.concatenate([prep_re, prep_im], axis=1))
    band_dev = SG // lax.axis_size("fcol")
    freqs = jnp.arange(band_dev * lax.axis_size("fcol"), dtype=jnp.int32)
    outputs = []
    for column in range(column_count):
        table_re, table_im = dft_table(gcol[:, None], band_offset[column] + freqs[None, :])
        whole_table = block_table(table_re, table_im)
        product = lax.dot_general(
            whole_table,
            prepared[column],
            (((0,), (1,)), ((), ())),
            preferred_element_type=jnp.float32,
        )
        outputs.append(
            product.reshape(2, band_dev * lax.axis_size("fcol"), facet).transpose(1, 0, 2)
        )
    summed = lax.psum_scatter(jnp.stack(outputs, axis=1), "fcol", scatter_dimension=0, tiled=True)
    banded = (summed / math.sqrt(facet * lax.axis_size("fcol"))).astype(jnp.bfloat16)
    chosen = jnp.take(banded, sub_column, axis=1)
    right_side = chosen.transpose(1, 2, 3, 0).reshape(sub_count, 2 * facet, band_dev)
    table_re, table_im = dft_table(
        row_ids[None, :, None], sub_row_offset[:, None, None] + freq_base[None, None, :]
    )
    left_real = jnp.concatenate([table_re, -table_im], axis=1)
    left_imag = jnp.concatenate([table_im, table_re], axis=1)
    left_side = jnp.stack([left_real, left_imag], axis=2)
    term = jnp.einsum("kxcu,kxv->kcuv", left_side, right_side, preferred_element_type=jnp.float32)
    term = term * (1.0 / math.sqrt(facet * lax.axis_size("frow")))
    return lax.psum_scatter(term, "frow", scatter_dimension=2, tiled=True)


MESH = pl.DeviceIdType.MESH
ROWS = 16


def unit_phasor(index):
    quadrant = (index + IMAGE // 8) >> 14
    t = (index - (quadrant << 14)).astype(jnp.float32) * (2.0 * math.pi / IMAGE)
    s = t * t
    sine = t * (1.0 + s * (-1 / 6 + s * (1 / 120 + s * (-1 / 5040 + s * (1 / 362880)))))
    cosine = 1.0 + s * (
        -1 / 2 + s * (1 / 24 + s * (-1 / 720 + s * (1 / 40320 + s * (-1 / 3628800))))
    )
    odd = (quadrant & 1) == 1
    real = jnp.where(odd, sine, cosine)
    imag = jnp.where(odd, cosine, sine)
    real = jnp.where(((quadrant + 1) & 2) == 2, -real, real)
    imag = jnp.where((quadrant & 2) == 2, imag, -imag)
    return real, imag


def residue(first, second):
    return (first * second) & (IMAGE - 1)


def coord_square(coords):
    unit = (coords & (IMAGE - 1)).astype(jnp.float32) / IMAGE - 0.5
    return unit * unit


def times(a, b):
    return a[0] * b[0] - a[1] * b[1], a[0] * b[1] + a[1] * b[0]


def iota(shape, axis):
    return lax.broadcasted_iota(jnp.int32, shape, axis)


def fused_kernel(
    dims,
    image_ref, wrow_ref, wcol_ref, w_ref, row_off_ref, col_off_ref, band_ref, sub_off_ref, sub_col_ref,
    out_ref,
    send, got, wsend, wgot, left, right, band, rtab, coarse, fine, phases,
    part, recv1, sum1, recv2, sum2, recv3,
    isend, irecv, s1, r1, s2, r2, s3, r3,
):
    n_side, n_z, n_sub, facet, sg = dims
    r = lax.axis_index("frow")
    c = lax.axis_index("fcol")
    x, core = c // 2, c % 2
    z, y = r // n_side, r % n_side
    block = sg // (2 * n_side)
    urows = sg // (n_side * n_z)
    nv = sg // 2
    partner = (r, c + 1 - 2 * core)
    first = x * (1 - core) + y * core
    second = y * (1 - core) + x * core

    def place(a, b, zz):
        xx = a * (1 - core) + b * core
        yy = b * (1 - core) + a * core
        return (zz * n_side + yy, xx * 2 + core)

    firsts = [(first + d) % n_side for d in range(1, n_side)]
    seconds = [(second + d) % n_side for d in range(1, n_side)]
    zs = [(z + d) % n_z for d in range(1, n_z)]
    peers = (
        [partner]
        + [place(a, second, z) for a in firsts]
        + [place(first, b, z) for b in seconds]
        + [place(first, second, q) for q in zs]
    )
    barrier = pltpu.get_barrier_semaphore()
    for peer in peers:
        pl.semaphore_signal(barrier, inc=1, device_id=peer, device_id_type=MESH)

    send[...] = image_ref[...].astype(jnp.float32)
    wsend[...] = jnp.broadcast_to(wcol_ref[...], wsend.shape)

    lane = iota((1, facet), 1)
    gcol = [col_off_ref[c] + lane, col_off_ref[partner[1]] + lane]
    grow = row_off_ref[r] + lane
    columns = [sub_col_ref[k] for k in range(n_sub)]

    row_id = iota((phases.shape[1], facet), 0)
    angle = jnp.zeros((phases.shape[1], facet), jnp.float32)
    for k in range(n_sub):
        w = w_ref[columns[k]]
        for f, coords in enumerate(gcol + [grow]):
            angle = jnp.where(row_id == 3 * k + f, w * coord_square(coords), angle)
    phases[0] = jnp.cos(angle)
    phases[1] = jnp.sin(angle)

    def write_fine(coords):
        q = unit_phasor(residue(coords, iota((ROWS, facet), 0)))
        fine[0] = q[0]
        fine[1] = q[1]

    def write_coarse(coords, freqs, gain, row):
        p = times(
            unit_phasor(residue(coords, freqs)),
            (phases[0, row : row + 1, :] * gain, phases[1, row : row + 1, :] * gain),
        )
        coarse[0, : freqs.shape[0]] = p[0]
        coarse[1, : freqs.shape[0]] = p[1]

    def entries(h):
        re, im = times(
            (coarse[0, pl.ds(h, 1), :], coarse[1, pl.ds(h, 1), :]), (fine[0], fine[1])
        )
        return re.astype(jnp.bfloat16), im.astype(jnp.bfloat16)

    def build_columns(f):
        write_fine(gcol[f])
        gain = wcol_ref[...] if f == 0 else wgot[0:1, :]
        at = 2 * facet * f
        for k in range(n_sub):
            index = iota((nv // ROWS, facet), 0) * ROWS
            v = block * (2 * (index // block) + core) + index % block
            write_coarse(gcol[f], band_ref[columns[k]] + v, gain, 3 * k + f)

            def body(h, carry, k=k):
                re, im = entries(h)
                top = pl.ds(pl.multiple_of(h * ROWS, ROWS), ROWS)
                low = pl.ds(pl.multiple_of(nv + h * ROWS, ROWS), ROWS)
                right[k, top, at : at + facet] = re
                right[k, top, at + facet : at + 2 * facet] = -im
                right[k, low, at : at + facet] = im
                right[k, low, at + facet : at + 2 * facet] = re
                return carry

            lax.fori_loop(0, nv // ROWS, body, 0)

    def build_rows():
        write_fine(grow)
        for k in range(n_sub):
            index = iota((sg // ROWS, facet), 0) * ROWS
            per = sg // n_side
            u = urows * (n_side * (index % per // urows) + index // per) + index % urows
            gain = wrow_ref[...] * dims_scale
            write_coarse(grow, sub_off_ref[k] + u, gain, 3 * k + 2)

            def body(h, carry, k=k):
                re, im = entries(h)
                at = pl.ds(pl.multiple_of(h * ROWS, ROWS), ROWS)
                rtab[k, 0, at, :facet] = re
                rtab[k, 0, at, facet:] = -im
                rtab[k, 1, at, :facet] = im
                rtab[k, 1, at, facet:] = re
                return carry

            lax.fori_loop(0, sg // ROWS, body, 0)

    dims_scale = 1.0 / math.sqrt(facet * lax.axis_size("fcol")) / math.sqrt(facet * lax.axis_size("frow"))

    def remote(src, dst, a, b, peer):
        return pltpu.make_async_remote_copy(
            src_ref=src, dst_ref=dst, send_sem=a, recv_sem=b, device_id=peer, device_id_type=MESH
        )

    pl.semaphore_wait(barrier, len(peers))
    wcopy = remote(wsend, wgot, isend.at[0], irecv.at[0], partner)
    icopy = remote(send, got, isend.at[1], irecv.at[1], partner)
    wcopy.start()
    icopy.start()
    left[:, :facet] = image_ref[0]
    left[:, facet : 2 * facet] = image_ref[1]
    build_columns(0)
    wcopy.wait()
    build_columns(1)
    build_rows()
    icopy.wait()
    left[:, 2 * facet : 3 * facet] = got[0].astype(jnp.bfloat16)
    left[:, 3 * facet :] = got[1].astype(jnp.bfloat16)

    n_chunk = 2 * n_sub
    copies1, copies2, copies3 = [], [], []
    step = 128
    for k in range(n_sub):

        def contract(i, carry, k=k):
            at = pl.ds(pl.multiple_of(i * step, step), step)
            value = lax.dot_general(
                left[at, :], right[k], (((1,), (1,)), ((), ())), preferred_element_type=jnp.float32
            ).astype(jnp.bfloat16)
            band[k, at, :] = value[:, :nv]
            band[k, pl.ds(pl.multiple_of(facet + i * step, step), step), :] = value[:, nv:]
            return carry

        lax.fori_loop(0, facet // step, contract, 0)
        for half in range(2):
            ch = 2 * k + half
            rows = sg // n_side
            for yb in range(n_side):
                value = jnp.dot(
                    rtab[k, half, yb * rows : (yb + 1) * rows, :],
                    band[k],
                    preferred_element_type=jnp.float32,
                )
                for xb in range(n_side):
                    a = xb * (1 - core) + yb * core
                    b = yb * (1 - core) + xb * core
                    part[ch, a, b] = value[:, xb * block : (xb + 1) * block]
            group = [
                remote(part.at[ch, a], recv1.at[ch, d], s1.at[ch, d], r1.at[ch, d], place(a, second, z))
                for d, a in enumerate(firsts)
            ]
            for copy in group:
                copy.start()
            copies1.append(group)

    for t in range(n_chunk + 1):
        if t < n_chunk:
            ch = t
            for copy in copies1[ch]:
                copy.wait_recv()
            total = part[ch, first]
            for d in range(n_side - 1):
                total = total + recv1[ch, d]
            sum1[ch] = total
            group = [
                remote(sum1.at[ch, b], recv2.at[ch, d], s2.at[ch, d], r2.at[ch, d], place(first, b, z))
                for d, b in enumerate(seconds)
            ]
            for copy in group:
                copy.start()
            copies2.append(group)
        if t >= 1:
            ch = t - 1
            for copy in copies2[ch]:
                copy.wait_recv()
            total = sum1[ch, second]
            for d in range(n_side - 1):
                total = total + recv2[ch, d]
            sum2[ch] = total.reshape(n_z, urows, block)
            group = [
                remote(sum2.at[ch, q], recv3.at[ch, d], s3.at[ch, d], r3.at[ch, d], place(first, second, q))
                for d, q in enumerate(zs)
            ]
            for copy in group:
                copy.start()
            copies3.append(group)
    for ch in range(n_chunk):
        for copy in copies3[ch]:
            copy.wait_recv()
        total = sum2[ch, z]
        for d in range(n_z - 1):
            total = total + recv3[ch, d]
        out_ref[ch // 2, ch % 2] = total
    for group in copies1 + copies2 + copies3:
        for copy in group:
            copy.wait_send()


def fused_local(n_side, n_z, image, window_rows, window_cols, *scalars):
    facet = image.shape[1]
    n_sub = scalars[4].shape[0]
    n_chunk = 2 * n_sub
    block = SG // (2 * n_side)
    urows = SG // (n_side * n_z)
    rows = SG // n_side
    f32, b16 = jnp.float32, jnp.bfloat16
    vmem = pl.BlockSpec(memory_space=pltpu.VMEM)
    smem = pl.BlockSpec(memory_space=pltpu.SMEM)
    dma = pltpu.SemaphoreType.DMA
    return pl.pallas_call(
        functools.partial(fused_kernel, (n_side, n_z, n_sub, facet, SG)),
        out_shape=jax.ShapeDtypeStruct((n_sub, 2, urows, block), f32),
        in_specs=[vmem] * 3 + [smem] * 6,
        out_specs=vmem,
        scratch_shapes=[
            pltpu.VMEM(image.shape, f32),
            pltpu.VMEM(image.shape, f32),
            pltpu.VMEM((8, facet), f32),
            pltpu.VMEM((8, facet), f32),
            pltpu.VMEM((facet, 4 * facet), b16),
            pltpu.VMEM((n_sub, SG, 4 * facet), b16),
            pltpu.VMEM((n_sub, 2 * facet, SG // 2), b16),
            pltpu.VMEM((n_sub, 2, SG, 2 * facet), b16),
            pltpu.VMEM((2, SG // ROWS, facet), f32),
            pltpu.VMEM((2, ROWS, facet), f32),
            pltpu.VMEM((2, -(-3 * n_sub // 8) * 8, facet), f32),
            pltpu.VMEM((n_chunk, n_side, n_side, rows, block), f32),
            pltpu.VMEM((n_chunk, n_side - 1, n_side, rows, block), f32),
            pltpu.VMEM((n_chunk, n_side, rows, block), f32),
            pltpu.VMEM((n_chunk, n_side - 1, rows, block), f32),
            pltpu.VMEM((n_chunk, n_z, urows, block), f32),
            pltpu.VMEM((n_chunk, n_z - 1, urows, block), f32),
            dma((2,)),
            dma((2,)),
            dma((n_chunk, n_side - 1)),
            dma((n_chunk, n_side - 1)),
            dma((n_chunk, n_side - 1)),
            dma((n_chunk, n_side - 1)),
            dma((n_chunk, n_z - 1)),
            dma((n_chunk, n_z - 1)),
        ],
        compiler_params=pltpu.CompilerParams(
            collective_id=0, has_side_effects=True, vmem_limit_bytes=56 << 20
        ),
    )(image, window_rows.reshape(1, -1), window_cols.reshape(1, -1), *scalars)


def solution(mesh):
    n_side = mesh.shape["fcol"] // 2
    n_z = mesh.shape["frow"] // n_side
    tiled = (
        n_side >= 2
        and n_z >= 2
        and mesh.shape["fcol"] == 2 * n_side
        and mesh.shape["frow"] == n_z * n_side
        and SG % (2 * n_side * 128) == 0
        and SG % (n_side * n_z * ROWS) == 0
    )

    def local(image, *rest):
        if tiled and image.shape[1] == image.shape[2] and image.shape[1] % 128 == 0:
            return fused_local(n_side, n_z, image, *rest)
        return general_local(image, *rest)

    placed = (P(None, "frow", "fcol"), P("frow"), P("fcol"), P(), P(), P(), P(), P(), P())
    return jax.shard_map(
        local, mesh=mesh, in_specs=placed, out_specs=P(None, None, "frow", "fcol"), check_vma=False
    )
```

```python
import functools
import math

import jax
import jax.numpy as jnp
from jax import lax
from jax.experimental import pallas as pl
from jax.experimental.pallas import tpu as pltpu
from jax.sharding import PartitionSpec as P

SG = 512
IMAGE = 65536


def phase_index(first, second):
    high = first * (second // 256) % 256 * 256
    return (high + first * (second % 256)) % 65536


def dft_table(coords, freqs):
    angle = phase_index(coords, freqs).astype(jnp.float32) * (2.0 * math.pi / IMAGE)
    return (jnp.cos(angle).astype(jnp.bfloat16), (-jnp.sin(angle)).astype(jnp.bfloat16))


def coord_unit(coords):
    return (coords % IMAGE).astype(jnp.float32) / IMAGE - 0.5


def block_table(table_re, table_im):
    upper = jnp.concatenate([table_re, table_im], axis=1)
    lower = jnp.concatenate([-table_im, table_re], axis=1)
    return jnp.concatenate([upper, lower], axis=0)


def general_local(
    image,
    window_rows,
    window_cols,
    w_terms,
    facet_row_offset,
    facet_col_offset,
    band_offset,
    sub_row_offset,
    sub_column,
):
    facet = image.shape[1]
    column_count = band_offset.shape[0]
    sub_count = sub_row_offset.shape[0]
    frow_index = lax.axis_index("frow")
    fcol_index = lax.axis_index("fcol")
    freq_base = jnp.arange(SG, dtype=jnp.int32)
    gcol = facet_col_offset[fcol_index] + jnp.arange(image.shape[2], dtype=jnp.int32)
    mcoord = coord_unit(gcol)
    row_base = facet_row_offset[frow_index]
    row_ids = row_base + jnp.arange(facet, dtype=jnp.int32)
    radius = coord_unit(row_ids)[:, None] ** 2 + mcoord[None, :] ** 2
    scale = window_rows[:, None] * window_cols[None, :]
    first = image[0].astype(jnp.float32) * scale
    second = image[1].astype(jnp.float32) * scale
    prepared = []
    for column in range(column_count):
        angle = w_terms[column] * radius
        cosine = jnp.cos(angle)
        sine = jnp.sin(angle)
        prep_re = (first * cosine - second * sine).astype(jnp.bfloat16)
        prep_im = (first * sine + second * cosine).astype(jnp.bfloat16)
        prepared.append(jnp.concatenate([prep_re, prep_im], axis=1))
    band_dev = SG // lax.axis_size("fcol")
    freqs = jnp.arange(band_dev * lax.axis_size("fcol"), dtype=jnp.int32)
    outputs = []
    for column in range(column_count):
        table_re, table_im = dft_table(gcol[:, None], band_offset[column] + freqs[None, :])
        whole_table = block_table(table_re, table_im)
        product = lax.dot_general(
            whole_table,
            prepared[column],
            (((0,), (1,)), ((), ())),
            preferred_element_type=jnp.float32,
        )
        outputs.append(
            product.reshape(2, band_dev * lax.axis_size("fcol"), facet).transpose(1, 0, 2)
        )
    summed = lax.psum_scatter(jnp.stack(outputs, axis=1), "fcol", scatter_dimension=0, tiled=True)
    banded = (summed / math.sqrt(facet * lax.axis_size("fcol"))).astype(jnp.bfloat16)
    chosen = jnp.take(banded, sub_column, axis=1)
    right_side = chosen.transpose(1, 2, 3, 0).reshape(sub_count, 2 * facet, band_dev)
    table_re, table_im = dft_table(
        row_ids[None, :, None], sub_row_offset[:, None, None] + freq_base[None, None, :]
    )
    left_real = jnp.concatenate([table_re, -table_im], axis=1)
    left_imag = jnp.concatenate([table_im, table_re], axis=1)
    left_side = jnp.stack([left_real, left_imag], axis=2)
    term = jnp.einsum("kxcu,kxv->kcuv", left_side, right_side, preferred_element_type=jnp.float32)
    term = term * (1.0 / math.sqrt(facet * lax.axis_size("frow")))
    return lax.psum_scatter(term, "frow", scatter_dimension=2, tiled=True)


MESH = pl.DeviceIdType.MESH
ROWS = 16
PARTS = 2


def unit_phasor(index):
    quadrant = (index + IMAGE // 8) >> 14
    t = (index - (quadrant << 14)).astype(jnp.float32) * (2.0 * math.pi / IMAGE)
    s = t * t
    sine = t * (1.0 + s * (-1 / 6 + s * (1 / 120 + s * (-1 / 5040 + s * (1 / 362880)))))
    cosine = 1.0 + s * (
        -1 / 2 + s * (1 / 24 + s * (-1 / 720 + s * (1 / 40320 + s * (-1 / 3628800))))
    )
    odd = (quadrant & 1) == 1
    real = jnp.where(odd, sine, cosine)
    imag = jnp.where(odd, cosine, sine)
    real = jnp.where(((quadrant + 1) & 2) == 2, -real, real)
    imag = jnp.where((quadrant & 2) == 2, imag, -imag)
    return real, imag


def residue(first, second):
    return (first * second) & (IMAGE - 1)


def coord_square(coords):
    unit = (coords & (IMAGE - 1)).astype(jnp.float32) / IMAGE - 0.5
    return unit * unit


def times(a, b):
    return a[0] * b[0] - a[1] * b[1], a[0] * b[1] + a[1] * b[0]


def iota(shape, axis):
    return lax.broadcasted_iota(jnp.int32, shape, axis)


def fused_kernel(
    dims,
    image_hbm, wrow_ref, wcol_ref, w_ref, row_off_ref, col_off_ref, band_ref, sub_off_ref, sub_col_ref,
    out_ref,
    left, right, hown, hsend, hgot, band, rtab, coarse, fine, phases,
    part, recv1, sum1, recv2, sum2, recv3,
    lsem, isend, irecv, s1, r1, s2, r2, s3, r3,
):
    n_side, n_z, n_sub, facet, sg = dims
    r = lax.axis_index("frow")
    c = lax.axis_index("fcol")
    x, core = c // 2, c % 2
    z, y = r // n_side, r % n_side
    block = sg // (2 * n_side)
    urows = sg // (n_side * n_z)
    up = urows // PARTS
    nv = sg // 2
    partner = (r, c + 1 - 2 * core)
    first = x * (1 - core) + y * core
    second = y * (1 - core) + x * core

    def place(a, b, zz):
        xx = a * (1 - core) + b * core
        yy = b * (1 - core) + a * core
        return (zz * n_side + yy, xx * 2 + core)

    firsts = [(first + d) % n_side for d in range(1, n_side)]
    seconds = [(second + d) % n_side for d in range(1, n_side)]
    zs = [(z + d) % n_z for d in range(1, n_z)]
    peers = (
        [place(first, second, q) for q in zs]
        + [place(a, second, z) for a in firsts]
        + [place(first, b, z) for b in seconds]
        + [partner]
    )
    barrier = pltpu.get_barrier_semaphore()
    for peer in peers:
        pl.semaphore_signal(barrier, inc=1, device_id=peer, device_id_type=MESH)

    loads = [
        pltpu.make_async_copy(
            image_hbm.at[i], left.at[:, i * facet : (i + 1) * facet], lsem.at[i]
        )
        for i in range(2)
    ]
    for load in loads:
        load.start()

    lane = iota((1, facet), 1)
    gcol = col_off_ref[c] + lane
    grow = row_off_ref[r] + lane
    columns = [sub_col_ref[k] for k in range(n_sub)]

    row_id = iota((phases.shape[1], facet), 0)
    angle = jnp.zeros((phases.shape[1], facet), jnp.float32)
    for k in range(n_sub):
        w = w_ref[columns[k]]
        for f, coords in enumerate((gcol, grow)):
            angle = jnp.where(row_id == 2 * k + f, w * coord_square(coords), angle)
    phases[0] = jnp.cos(angle)
    phases[1] = jnp.sin(angle)

    def write_fine(coords):
        q = unit_phasor(residue(coords, iota((ROWS, facet), 0)))
        fine[0] = q[0]
        fine[1] = q[1]

    def write_coarse(coords, freqs, gain, row):
        p = times(
            unit_phasor(residue(coords, freqs)),
            (phases[0, row : row + 1, :] * gain, phases[1, row : row + 1, :] * gain),
        )
        coarse[0] = p[0]
        coarse[1] = p[1]

    def entries(h):
        re, im = times(
            (coarse[0, pl.ds(h, 1), :], coarse[1, pl.ds(h, 1), :]), (fine[0], fine[1])
        )
        return re.astype(jnp.bfloat16), im.astype(jnp.bfloat16)

    def build_columns(k):
        index = iota((sg // ROWS, facet), 0) * ROWS
        owner = (core + index // nv) % 2
        inner = index % nv
        v = block * (2 * (inner // block) + owner) + inner % block
        write_coarse(gcol, band_ref[columns[k]] + v, wcol_ref[...], 2 * k)
        for side in range(2):

            def body(h, carry, side=side):
                re, im = entries(side * (nv // ROWS) + h)
                top = pl.ds(pl.multiple_of(h * ROWS, ROWS), ROWS)
                low = pl.ds(pl.multiple_of(nv + h * ROWS, ROWS), ROWS)
                right[side, k, top, :facet] = re
                right[side, k, top, facet:] = -im
                right[side, k, low, :facet] = im
                right[side, k, low, facet:] = re
                return carry

            lax.fori_loop(0, nv // ROWS, body, 0)

    def build_rows():
        write_fine(grow)
        for k in range(n_sub):
            index = iota((sg // ROWS, facet), 0) * ROWS
            inner = index % (sg // PARTS)
            per = up * n_z
            u = (
                urows * (n_side * (inner % per // up) + inner // per)
                + up * (index // (sg // PARTS))
                + index % up
            )
            write_coarse(grow, sub_off_ref[k] + u, wrow_ref[...] * scale, 2 * k + 1)

            def body(h, carry, k=k):
                re, im = entries(h)
                at = pl.ds(pl.multiple_of(h * ROWS, ROWS), ROWS)
                rtab[k, 0, at, :facet] = re
                rtab[k, 0, at, facet:] = -im
                rtab[k, 1, at, :facet] = im
                rtab[k, 1, at, facet:] = re
                return carry

            lax.fori_loop(0, sg // ROWS, body, 0)

    scale = 1.0 / math.sqrt(facet * lax.axis_size("fcol")) / math.sqrt(facet * lax.axis_size("frow"))

    def remote(src, dst, a, b, peer):
        return pltpu.make_async_remote_copy(
            src_ref=src, dst_ref=dst, send_sem=a, recv_sem=b, device_id=peer, device_id_type=MESH
        )

    write_fine(gcol)
    for k in range(n_sub):
        build_columns(k)
    for load in loads:
        load.wait()
    for k in range(n_sub):
        for side, target in ((1, hsend), (0, hown)):
            target[k] = lax.dot_general(
                left[...],
                right[side, k],
                (((1,), (1,)), ((), ())),
                preferred_element_type=jnp.float32,
            )
    pl.semaphore_wait(barrier, len(peers))
    swaps = [
        remote(hsend.at[k], hgot.at[k], isend.at[k], irecv.at[k], partner) for k in range(n_sub)
    ]
    for swap in swaps:
        swap.start()
    build_rows()

    n_chunk = 2 * n_sub * PARTS
    where = [(k, half, p) for k in range(n_sub) for half in range(2) for p in range(PARTS)]
    copies1, copies2, copies3 = [], [], []
    rows = up * n_z
    for ch, (k, half, p) in enumerate(where):
        if half == 0 and p == 0:
            swaps[k].wait_recv()
            for i in range(2):
                at = slice(i * nv, (i + 1) * nv)
                band[k, i * facet : (i + 1) * facet, :] = (hown[k, :, at] + hgot[k, :, at]).astype(
                    jnp.bfloat16
                )
        span = sg // PARTS
        value = jnp.dot(
            rtab[k, half, p * span : (p + 1) * span, :],
            band[k],
            preferred_element_type=jnp.float32,
        )
        for yb in range(n_side):
            for xb in range(n_side):
                a = xb * (1 - core) + yb * core
                b = yb * (1 - core) + xb * core
                part[ch, a, b] = value[yb * rows : (yb + 1) * rows, xb * block : (xb + 1) * block]
        group = [
            remote(part.at[ch, a], recv1.at[ch, d], s1.at[ch, d], r1.at[ch, d], place(a, second, z))
            for d, a in enumerate(firsts)
        ]
        for copy in group:
            copy.start()
        copies1.append(group)

    for t in range(n_chunk + 1):
        if t < n_chunk:
            ch = t
            for copy in copies1[ch]:
                copy.wait_recv()
            total = part[ch, first]
            for d in range(n_side - 1):
                total = total + recv1[ch, d]
            sum1[ch] = total
            group = [
                remote(sum1.at[ch, b], recv2.at[ch, d], s2.at[ch, d], r2.at[ch, d], place(first, b, z))
                for d, b in enumerate(seconds)
            ]
            for copy in group:
                copy.start()
            copies2.append(group)
        if t >= 1:
            ch = t - 1
            for copy in copies2[ch]:
                copy.wait_recv()
            total = sum1[ch, second]
            for d in range(n_side - 1):
                total = total + recv2[ch, d]
            sum2[ch] = total.reshape(n_z, up, block)
            group = [
                remote(sum2.at[ch, q], recv3.at[ch, d], s3.at[ch, d], r3.at[ch, d], place(first, second, q))
                for d, q in enumerate(zs)
            ]
            for copy in group:
                copy.start()
            copies3.append(group)
    for ch, (k, half, p) in enumerate(where):
        for copy in copies3[ch]:
            copy.wait_recv()
        total = sum2[ch, z]
        for d in range(n_z - 1):
            total = total + recv3[ch, d]
        out_ref[k, half, p * up : (p + 1) * up, :] = total
    for swap in swaps:
        swap.wait_send()
    for group in copies1 + copies2 + copies3:
        for copy in group:
            copy.wait_send()


def fused_local(n_side, n_z, image, window_rows, window_cols, *scalars):
    facet = image.shape[1]
    n_sub = scalars[4].shape[0]
    n_chunk = 2 * n_sub * PARTS
    block = SG // (2 * n_side)
    urows = SG // (n_side * n_z)
    up = urows // PARTS
    rows = up * n_z
    f32, b16 = jnp.float32, jnp.bfloat16
    vmem = pl.BlockSpec(memory_space=pltpu.VMEM)
    smem = pl.BlockSpec(memory_space=pltpu.SMEM)
    dma = pltpu.SemaphoreType.DMA
    return pl.pallas_call(
        functools.partial(fused_kernel, (n_side, n_z, n_sub, facet, SG)),
        out_shape=jax.ShapeDtypeStruct((n_sub, 2, urows, block), f32),
        in_specs=[pl.BlockSpec(memory_space=pl.ANY)] + [vmem] * 2 + [smem] * 6,
        out_specs=vmem,
        scratch_shapes=[
            pltpu.VMEM((facet, 2 * facet), b16),
            pltpu.VMEM((2, n_sub, SG, 2 * facet), b16),
            pltpu.VMEM((n_sub, facet, SG), f32),
            pltpu.VMEM((n_sub, facet, SG), f32),
            pltpu.VMEM((n_sub, facet, SG), f32),
            pltpu.VMEM((n_sub, 2 * facet, SG // 2), b16),
            pltpu.VMEM((n_sub, 2, SG, 2 * facet), b16),
            pltpu.VMEM((2, SG // ROWS, facet), f32),
            pltpu.VMEM((2, ROWS, facet), f32),
            pltpu.VMEM((2, -(-2 * n_sub // 8) * 8, facet), f32),
            pltpu.VMEM((n_chunk, n_side, n_side, rows, block), f32),
            pltpu.VMEM((n_chunk, n_side - 1, n_side, rows, block), f32),
            pltpu.VMEM((n_chunk, n_side, rows, block), f32),
            pltpu.VMEM((n_chunk, n_side - 1, rows, block), f32),
            pltpu.VMEM((n_chunk, n_z, up, block), f32),
            pltpu.VMEM((n_chunk, n_z - 1, up, block), f32),
            dma((2,)),
            dma((n_sub,)),
            dma((n_sub,)),
            dma((n_chunk, n_side - 1)),
            dma((n_chunk, n_side - 1)),
            dma((n_chunk, n_side - 1)),
            dma((n_chunk, n_side - 1)),
            dma((n_chunk, n_z - 1)),
            dma((n_chunk, n_z - 1)),
        ],
        compiler_params=pltpu.CompilerParams(
            collective_id=0, has_side_effects=True, vmem_limit_bytes=56 << 20
        ),
    )(image, window_rows.reshape(1, -1), window_cols.reshape(1, -1), *scalars)


def solution(mesh):
    n_side = mesh.shape["fcol"] // 2
    n_z = mesh.shape["frow"] // n_side
    tiled = (
        n_side >= 2
        and n_z >= 2
        and mesh.shape["fcol"] == 2 * n_side
        and mesh.shape["frow"] == n_z * n_side
        and SG % (2 * n_side * 128) == 0
        and SG % (n_side * n_z * ROWS * PARTS) == 0
    )

    def local(image, *rest):
        if tiled and image.shape[1] == image.shape[2] and image.shape[1] % 128 == 0:
            return fused_local(n_side, n_z, image, *rest)
        return general_local(image, *rest)

    placed = (P(None, "frow", "fcol"), P("frow"), P("fcol"), P(), P(), P(), P(), P(), P())
    return jax.shard_map(
        local, mesh=mesh, in_specs=placed, out_specs=P(None, None, "frow", "fcol"), check_vma=False
    )
```

```python
import functools
import math

import jax
import jax.numpy as jnp
from jax import lax
from jax.experimental import pallas as pl
from jax.experimental.pallas import tpu as pltpu
from jax.sharding import PartitionSpec as P

SG = 512
IMAGE = 65536


def phase_index(first, second):
    high = first * (second // 256) % 256 * 256
    return (high + first * (second % 256)) % 65536


def dft_table(coords, freqs):
    angle = phase_index(coords, freqs).astype(jnp.float32) * (2.0 * math.pi / IMAGE)
    return (jnp.cos(angle).astype(jnp.bfloat16), (-jnp.sin(angle)).astype(jnp.bfloat16))


def coord_unit(coords):
    return (coords % IMAGE).astype(jnp.float32) / IMAGE - 0.5


def block_table(table_re, table_im):
    upper = jnp.concatenate([table_re, table_im], axis=1)
    lower = jnp.concatenate([-table_im, table_re], axis=1)
    return jnp.concatenate([upper, lower], axis=0)


def general_local(
    image,
    window_rows,
    window_cols,
    w_terms,
    facet_row_offset,
    facet_col_offset,
    band_offset,
    sub_row_offset,
    sub_column,
):
    facet = image.shape[1]
    column_count = band_offset.shape[0]
    sub_count = sub_row_offset.shape[0]
    frow_index = lax.axis_index("frow")
    fcol_index = lax.axis_index("fcol")
    freq_base = jnp.arange(SG, dtype=jnp.int32)
    gcol = facet_col_offset[fcol_index] + jnp.arange(image.shape[2], dtype=jnp.int32)
    mcoord = coord_unit(gcol)
    row_base = facet_row_offset[frow_index]
    row_ids = row_base + jnp.arange(facet, dtype=jnp.int32)
    radius = coord_unit(row_ids)[:, None] ** 2 + mcoord[None, :] ** 2
    scale = window_rows[:, None] * window_cols[None, :]
    first = image[0].astype(jnp.float32) * scale
    second = image[1].astype(jnp.float32) * scale
    prepared = []
    for column in range(column_count):
        angle = w_terms[column] * radius
        cosine = jnp.cos(angle)
        sine = jnp.sin(angle)
        prep_re = (first * cosine - second * sine).astype(jnp.bfloat16)
        prep_im = (first * sine + second * cosine).astype(jnp.bfloat16)
        prepared.append(jnp.concatenate([prep_re, prep_im], axis=1))
    band_dev = SG // lax.axis_size("fcol")
    freqs = jnp.arange(band_dev * lax.axis_size("fcol"), dtype=jnp.int32)
    outputs = []
    for column in range(column_count):
        table_re, table_im = dft_table(gcol[:, None], band_offset[column] + freqs[None, :])
        whole_table = block_table(table_re, table_im)
        product = lax.dot_general(
            whole_table,
            prepared[column],
            (((0,), (1,)), ((), ())),
            preferred_element_type=jnp.float32,
        )
        outputs.append(
            product.reshape(2, band_dev * lax.axis_size("fcol"), facet).transpose(1, 0, 2)
        )
    summed = lax.psum_scatter(jnp.stack(outputs, axis=1), "fcol", scatter_dimension=0, tiled=True)
    banded = (summed / math.sqrt(facet * lax.axis_size("fcol"))).astype(jnp.bfloat16)
    chosen = jnp.take(banded, sub_column, axis=1)
    right_side = chosen.transpose(1, 2, 3, 0).reshape(sub_count, 2 * facet, band_dev)
    table_re, table_im = dft_table(
        row_ids[None, :, None], sub_row_offset[:, None, None] + freq_base[None, None, :]
    )
    left_real = jnp.concatenate([table_re, -table_im], axis=1)
    left_imag = jnp.concatenate([table_im, table_re], axis=1)
    left_side = jnp.stack([left_real, left_imag], axis=2)
    term = jnp.einsum("kxcu,kxv->kcuv", left_side, right_side, preferred_element_type=jnp.float32)
    term = term * (1.0 / math.sqrt(facet * lax.axis_size("frow")))
    return lax.psum_scatter(term, "frow", scatter_dimension=2, tiled=True)


MESH = pl.DeviceIdType.MESH
ROWS = 16
PARTS = 2


def unit_phasor(index):
    quadrant = (index + IMAGE // 8) >> 14
    t = (index - (quadrant << 14)).astype(jnp.float32) * (2.0 * math.pi / IMAGE)
    s = t * t
    sine = t * (1.0 + s * (-1 / 6 + s * (1 / 120 + s * (-1 / 5040 + s * (1 / 362880)))))
    cosine = 1.0 + s * (
        -1 / 2 + s * (1 / 24 + s * (-1 / 720 + s * (1 / 40320 + s * (-1 / 3628800))))
    )
    odd = (quadrant & 1) == 1
    real = jnp.where(odd, sine, cosine)
    imag = jnp.where(odd, cosine, sine)
    real = jnp.where(((quadrant + 1) & 2) == 2, -real, real)
    imag = jnp.where((quadrant & 2) == 2, imag, -imag)
    return real, imag


def residue(first, second):
    return (first * second) & (IMAGE - 1)


def coord_square(coords):
    unit = (coords & (IMAGE - 1)).astype(jnp.float32) / IMAGE - 0.5
    return unit * unit


def times(a, b):
    return a[0] * b[0] - a[1] * b[1], a[0] * b[1] + a[1] * b[0]


def iota(shape, axis):
    return lax.broadcasted_iota(jnp.int32, shape, axis)


def fused_kernel(
    dims,
    image_hbm, wrow_ref, wcol_ref, w_ref, row_off_ref, col_off_ref, band_ref, sub_off_ref, sub_col_ref,
    out_ref,
    left, right, hown, hsend, hgot, band, rtab, coarse, fine, phases,
    part, recv1, sum1, recv2, sum2, recv3, zpart, zrecv1, zsum1, zrecv2, zsum2, zrecv3,
    lsem, isend, irecv, s1, r1, s2, r2, s3, r3, t1, q1, t2, q2, t3, q3,
):
    n_side, n_z, n_sub, facet, sg = dims
    r = lax.axis_index("frow")
    c = lax.axis_index("fcol")
    x, core = c // 2, c % 2
    z, y = r // n_side, r % n_side
    block = sg // (2 * n_side)
    urows = sg // (n_side * n_z)
    up = urows // PARTS
    nv = sg // 2
    partner = (r, c + 1 - 2 * core)
    first = x * (1 - core) + y * core
    second = y * (1 - core) + x * core

    def place(a, b, zz):
        xx = a * (1 - core) + b * core
        yy = b * (1 - core) + a * core
        return (zz * n_side + yy, xx * 2 + core)

    firsts = [(first + d) % n_side for d in range(1, n_side)]
    seconds = [(second + d) % n_side for d in range(1, n_side)]
    zs = [(z + d) % n_z for d in range(1, n_z)]
    peers = (
        [place(first, second, q) for q in zs]
        + [place(a, second, z) for a in firsts]
        + [place(first, b, z) for b in seconds]
        + [partner]
    )
    barrier = pltpu.get_barrier_semaphore()
    for peer in peers:
        pl.semaphore_signal(barrier, inc=1, device_id=peer, device_id_type=MESH)

    loads = [
        pltpu.make_async_copy(
            image_hbm.at[i], left.at[:, i * facet : (i + 1) * facet], lsem.at[i]
        )
        for i in range(2)
    ]
    for load in loads:
        load.start()

    lane = iota((1, facet), 1)
    gcol = col_off_ref[c] + lane
    grow = row_off_ref[r] + lane
    columns = [sub_col_ref[k] for k in range(n_sub)]

    row_id = iota((phases.shape[1], facet), 0)
    angle = jnp.zeros((phases.shape[1], facet), jnp.float32)
    for k in range(n_sub):
        w = w_ref[columns[k]]
        for f, coords in enumerate((gcol, grow)):
            angle = jnp.where(row_id == 2 * k + f, w * coord_square(coords), angle)
    phases[0] = jnp.cos(angle)
    phases[1] = jnp.sin(angle)

    def write_fine(coords):
        q = unit_phasor(residue(coords, iota((ROWS, facet), 0)))
        fine[0] = q[0]
        fine[1] = q[1]

    def write_coarse(coords, freqs, gain, row):
        p = times(
            unit_phasor(residue(coords, freqs)),
            (phases[0, row : row + 1, :] * gain, phases[1, row : row + 1, :] * gain),
        )
        coarse[0] = p[0]
        coarse[1] = p[1]

    def entries(h):
        re, im = times(
            (coarse[0, pl.ds(h, 1), :], coarse[1, pl.ds(h, 1), :]), (fine[0], fine[1])
        )
        return re.astype(jnp.bfloat16), im.astype(jnp.bfloat16)

    def build_columns(k):
        index = iota((sg // ROWS, facet), 0) * ROWS
        owner = (core + index // nv) % 2
        inner = index % nv
        v = block * (2 * (inner // block) + owner) + inner % block
        write_coarse(gcol, band_ref[columns[k]] + v, wcol_ref[...], 2 * k)
        for side in range(2):

            def body(h, carry, side=side):
                re, im = entries(side * (nv // ROWS) + h)
                top = pl.ds(pl.multiple_of(h * ROWS, ROWS), ROWS)
                low = pl.ds(pl.multiple_of(nv + h * ROWS, ROWS), ROWS)
                right[side, k, top, :facet] = re
                right[side, k, top, facet:] = -im
                right[side, k, low, :facet] = im
                right[side, k, low, facet:] = re
                return carry

            lax.fori_loop(0, nv // ROWS, body, 0)

    def build_rows():
        write_fine(grow)
        for k in range(n_sub):
            index = iota((sg // ROWS, facet), 0) * ROWS
            inner = index % (sg // PARTS)
            per = up * n_z
            u = (
                urows * (n_side * (inner % per // up) + inner // per)
                + up * (index // (sg // PARTS))
                + index % up
            )
            write_coarse(grow, sub_off_ref[k] + u, wrow_ref[...] * scale, 2 * k + 1)

            def body(h, carry, k=k):
                re, im = entries(h)
                at = pl.ds(pl.multiple_of(h * ROWS, ROWS), ROWS)
                rtab[k, 0, at, :facet] = re
                rtab[k, 0, at, facet:] = -im
                rtab[k, 1, at, :facet] = im
                rtab[k, 1, at, facet:] = re
                return carry

            lax.fori_loop(0, sg // ROWS, body, 0)

    scale = 1.0 / math.sqrt(facet * lax.axis_size("fcol")) / math.sqrt(facet * lax.axis_size("frow"))

    def remote(src, dst, a, b, peer):
        return pltpu.make_async_remote_copy(
            src_ref=src, dst_ref=dst, send_sem=a, recv_sem=b, device_id=peer, device_id_type=MESH
        )

    write_fine(gcol)
    for k in range(n_sub):
        build_columns(k)
    build_rows()
    for load in loads:
        load.wait()
    for k in range(n_sub):
        for side, target in ((1, hsend), (0, hown)):
            target[k] = lax.dot_general(
                left[...],
                right[side, k],
                (((1,), (1,)), ((), ())),
                preferred_element_type=jnp.float32,
            )
    pl.semaphore_wait(barrier, len(peers))
    swaps = [
        remote(hsend.at[k], hgot.at[k], isend.at[k], irecv.at[k], partner) for k in range(n_sub)
    ]
    for swap in swaps:
        swap.start()
    n_chunk = 2 * n_sub * PARTS
    where = [(k, half, p) for k in range(n_sub) for half in range(2) for p in range(PARTS)]
    copies1, copies2, copies3 = [], [], []
    rows = up * n_z
    for ch, (k, half, p) in enumerate(where):
        if half == 0 and p == 0:
            swaps[k].wait_recv()
            for i in range(2):
                at = slice(i * nv, (i + 1) * nv)
                band[k, i * facet : (i + 1) * facet, :] = (hown[k, :, at] + hgot[k, :, at]).astype(
                    jnp.bfloat16
                )
        span = sg // PARTS
        value = jnp.dot(
            rtab[k, half, p * span : (p + 1) * span, :],
            band[k],
            preferred_element_type=jnp.float32,
        )
        for yb in range(n_side):
            for xb in range(n_side):
                a = xb * (1 - core) + yb * core
                b = yb * (1 - core) + xb * core
                tile = value[yb * rows : (yb + 1) * rows, xb * block : (xb + 1) * block]
                if ch == 0:
                    for zz in range(n_z):
                        zpart[zz, a, b] = tile[zz * up : (zz + 1) * up]
                else:
                    part[ch, a, b] = tile
        if ch == 0:
            zcopies = [
                [
                    remote(zpart.at[q], zrecv1.at[d], t1.at[d], q1.at[d], place(first, second, q))
                    for d, q in enumerate(zs)
                ]
            ]
            for copy in zcopies[0]:
                copy.start()
            continue
        group = [
            remote(part.at[ch, a], recv1.at[ch, d], s1.at[ch, d], r1.at[ch, d], place(a, second, z))
            for d, a in enumerate(firsts)
        ]
        for copy in group:
            copy.start()
        copies1.append(group)

    def advance(group, own, arrived):
        for copy in group:
            copy.wait_recv()
        total = own
        for d in range(len(group)):
            total = total + arrived[d]
        return total

    def launch(group):
        for copy in group:
            copy.start()
        return group

    for ch in range(1, n_chunk + 1):
        if ch < n_chunk:
            sum1[ch] = advance(copies1[ch - 1], part[ch, first], recv1.at[ch])
            copies2.append(
                launch(
                    [
                        remote(sum1.at[ch, b], recv2.at[ch, d], s2.at[ch, d], r2.at[ch, d], place(first, b, z))
                        for d, b in enumerate(seconds)
                    ]
                )
            )
        if ch == n_chunk // 2:
            zsum1[...] = advance(zcopies[0], zpart[z], zrecv1)
            zcopies.append(
                launch(
                    [
                        remote(zsum1.at[a], zrecv2.at[d], t2.at[d], q2.at[d], place(a, second, z))
                        for d, a in enumerate(firsts)
                    ]
                )
            )
        if ch >= 2:
            done = ch - 1
            total = advance(copies2[done - 1], sum1[done, second], recv2.at[done])
            sum2[done] = total.reshape(n_z, up, block)
            copies3.append(
                launch(
                    [
                        remote(sum2.at[done, q], recv3.at[done, d], s3.at[done, d], r3.at[done, d], place(first, second, q))
                        for d, q in enumerate(zs)
                    ]
                )
            )
    zsum2[...] = advance(zcopies[1], zsum1[first], zrecv2)
    zcopies.append(
        launch(
            [
                remote(zsum2.at[b], zrecv3.at[d], t3.at[d], q3.at[d], place(first, b, z))
                for d, b in enumerate(seconds)
            ]
        )
    )
    for ch, (k, half, p) in enumerate(where):
        if ch > 0:
            total = advance(copies3[ch - 1], sum2[ch, z], recv3.at[ch])
            out_ref[k, half, p * up : (p + 1) * up, :] = total
    out_ref[0, 0, :up, :] = advance(zcopies[2], zsum2[second], zrecv3)
    for swap in swaps:
        swap.wait_send()
    for group in copies1 + copies2 + copies3 + zcopies:
        for copy in group:
            copy.wait_send()


def fused_local(n_side, n_z, image, window_rows, window_cols, *scalars):
    facet = image.shape[1]
    n_sub = scalars[4].shape[0]
    n_chunk = 2 * n_sub * PARTS
    block = SG // (2 * n_side)
    urows = SG // (n_side * n_z)
    up = urows // PARTS
    rows = up * n_z
    f32, b16 = jnp.float32, jnp.bfloat16
    vmem = pl.BlockSpec(memory_space=pltpu.VMEM)
    smem = pl.BlockSpec(memory_space=pltpu.SMEM)
    dma = pltpu.SemaphoreType.DMA
    return pl.pallas_call(
        functools.partial(fused_kernel, (n_side, n_z, n_sub, facet, SG)),
        out_shape=jax.ShapeDtypeStruct((n_sub, 2, urows, block), f32),
        in_specs=[pl.BlockSpec(memory_space=pl.ANY)] + [vmem] * 2 + [smem] * 6,
        out_specs=vmem,
        scratch_shapes=[
            pltpu.VMEM((facet, 2 * facet), b16),
            pltpu.VMEM((2, n_sub, SG, 2 * facet), b16),
            pltpu.VMEM((n_sub, facet, SG), f32),
            pltpu.VMEM((n_sub, facet, SG), f32),
            pltpu.VMEM((n_sub, facet, SG), f32),
            pltpu.VMEM((n_sub, 2 * facet, SG // 2), b16),
            pltpu.VMEM((n_sub, 2, SG, 2 * facet), b16),
            pltpu.VMEM((2, SG // ROWS, facet), f32),
            pltpu.VMEM((2, ROWS, facet), f32),
            pltpu.VMEM((2, -(-2 * n_sub // 8) * 8, facet), f32),
            pltpu.VMEM((n_chunk, n_side, n_side, rows, block), f32),
            pltpu.VMEM((n_chunk, n_side - 1, n_side, rows, block), f32),
            pltpu.VMEM((n_chunk, n_side, rows, block), f32),
            pltpu.VMEM((n_chunk, n_side - 1, rows, block), f32),
            pltpu.VMEM((n_chunk, n_z, up, block), f32),
            pltpu.VMEM((n_chunk, n_z - 1, up, block), f32),
            pltpu.VMEM((n_z, n_side, n_side, up, block), f32),
            pltpu.VMEM((n_z - 1, n_side, n_side, up, block), f32),
            pltpu.VMEM((n_side, n_side, up, block), f32),
            pltpu.VMEM((n_side - 1, n_side, up, block), f32),
            pltpu.VMEM((n_side, up, block), f32),
            pltpu.VMEM((n_side - 1, up, block), f32),
            dma((2,)),
            dma((n_sub,)),
            dma((n_sub,)),
            dma((n_chunk, n_side - 1)),
            dma((n_chunk, n_side - 1)),
            dma((n_chunk, n_side - 1)),
            dma((n_chunk, n_side - 1)),
            dma((n_chunk, n_z - 1)),
            dma((n_chunk, n_z - 1)),
            dma((n_z - 1,)),
            dma((n_z - 1,)),
            dma((n_side - 1,)),
            dma((n_side - 1,)),
            dma((n_side - 1,)),
            dma((n_side - 1,)),
        ],
        compiler_params=pltpu.CompilerParams(
            collective_id=0, has_side_effects=True, vmem_limit_bytes=56 << 20
        ),
    )(image, window_rows.reshape(1, -1), window_cols.reshape(1, -1), *scalars)


def solution(mesh):
    n_side = mesh.shape["fcol"] // 2
    n_z = mesh.shape["frow"] // n_side
    tiled = (
        n_side >= 2
        and n_z >= 2
        and mesh.shape["fcol"] == 2 * n_side
        and mesh.shape["frow"] == n_z * n_side
        and SG % (2 * n_side * 128) == 0
        and SG % (n_side * n_z * ROWS * PARTS) == 0
    )

    def local(image, *rest):
        if tiled and image.shape[1] == image.shape[2] and image.shape[1] % 128 == 0:
            return fused_local(n_side, n_z, image, *rest)
        return general_local(image, *rest)

    placed = (P(None, "frow", "fcol"), P("frow"), P("fcol"), P(), P(), P(), P(), P(), P())
    return jax.shard_map(
        local, mesh=mesh, in_specs=placed, out_specs=P(None, None, "frow", "fcol"), check_vma=False
    )
```

```python
import functools
import math

import jax
import jax.numpy as jnp
from jax import lax
from jax.experimental import pallas as pl
from jax.experimental.pallas import tpu as pltpu
from jax.sharding import PartitionSpec as P

SG = 512
IMAGE = 65536


def phase_index(first, second):
    high = first * (second // 256) % 256 * 256
    return (high + first * (second % 256)) % 65536


def dft_table(coords, freqs):
    angle = phase_index(coords, freqs).astype(jnp.float32) * (2.0 * math.pi / IMAGE)
    return (jnp.cos(angle).astype(jnp.bfloat16), (-jnp.sin(angle)).astype(jnp.bfloat16))


def coord_unit(coords):
    return (coords % IMAGE).astype(jnp.float32) / IMAGE - 0.5


def block_table(table_re, table_im):
    upper = jnp.concatenate([table_re, table_im], axis=1)
    lower = jnp.concatenate([-table_im, table_re], axis=1)
    return jnp.concatenate([upper, lower], axis=0)


def general_local(
    image,
    window_rows,
    window_cols,
    w_terms,
    facet_row_offset,
    facet_col_offset,
    band_offset,
    sub_row_offset,
    sub_column,
):
    facet = image.shape[1]
    column_count = band_offset.shape[0]
    sub_count = sub_row_offset.shape[0]
    frow_index = lax.axis_index("frow")
    fcol_index = lax.axis_index("fcol")
    freq_base = jnp.arange(SG, dtype=jnp.int32)
    gcol = facet_col_offset[fcol_index] + jnp.arange(image.shape[2], dtype=jnp.int32)
    mcoord = coord_unit(gcol)
    row_base = facet_row_offset[frow_index]
    row_ids = row_base + jnp.arange(facet, dtype=jnp.int32)
    radius = coord_unit(row_ids)[:, None] ** 2 + mcoord[None, :] ** 2
    scale = window_rows[:, None] * window_cols[None, :]
    first = image[0].astype(jnp.float32) * scale
    second = image[1].astype(jnp.float32) * scale
    prepared = []
    for column in range(column_count):
        angle = w_terms[column] * radius
        cosine = jnp.cos(angle)
        sine = jnp.sin(angle)
        prep_re = (first * cosine - second * sine).astype(jnp.bfloat16)
        prep_im = (first * sine + second * cosine).astype(jnp.bfloat16)
        prepared.append(jnp.concatenate([prep_re, prep_im], axis=1))
    band_dev = SG // lax.axis_size("fcol")
    freqs = jnp.arange(band_dev * lax.axis_size("fcol"), dtype=jnp.int32)
    outputs = []
    for column in range(column_count):
        table_re, table_im = dft_table(gcol[:, None], band_offset[column] + freqs[None, :])
        whole_table = block_table(table_re, table_im)
        product = lax.dot_general(
            whole_table,
            prepared[column],
            (((0,), (1,)), ((), ())),
            preferred_element_type=jnp.float32,
        )
        outputs.append(
            product.reshape(2, band_dev * lax.axis_size("fcol"), facet).transpose(1, 0, 2)
        )
    summed = lax.psum_scatter(jnp.stack(outputs, axis=1), "fcol", scatter_dimension=0, tiled=True)
    banded = (summed / math.sqrt(facet * lax.axis_size("fcol"))).astype(jnp.bfloat16)
    chosen = jnp.take(banded, sub_column, axis=1)
    right_side = chosen.transpose(1, 2, 3, 0).reshape(sub_count, 2 * facet, band_dev)
    table_re, table_im = dft_table(
        row_ids[None, :, None], sub_row_offset[:, None, None] + freq_base[None, None, :]
    )
    left_real = jnp.concatenate([table_re, -table_im], axis=1)
    left_imag = jnp.concatenate([table_im, table_re], axis=1)
    left_side = jnp.stack([left_real, left_imag], axis=2)
    term = jnp.einsum("kxcu,kxv->kcuv", left_side, right_side, preferred_element_type=jnp.float32)
    term = term * (1.0 / math.sqrt(facet * lax.axis_size("frow")))
    return lax.psum_scatter(term, "frow", scatter_dimension=2, tiled=True)


MESH = pl.DeviceIdType.MESH
ROWS = 16
PARTS = 2


def unit_phasor(index):
    quadrant = (index + IMAGE // 8) >> 14
    t = (index - (quadrant << 14)).astype(jnp.float32) * (2.0 * math.pi / IMAGE)
    s = t * t
    sine = t * (1.0 + s * (-1 / 6 + s * (1 / 120 + s * (-1 / 5040 + s * (1 / 362880)))))
    cosine = 1.0 + s * (
        -1 / 2 + s * (1 / 24 + s * (-1 / 720 + s * (1 / 40320 + s * (-1 / 3628800))))
    )
    odd = (quadrant & 1) == 1
    real = jnp.where(odd, sine, cosine)
    imag = jnp.where(odd, cosine, sine)
    real = jnp.where(((quadrant + 1) & 2) == 2, -real, real)
    imag = jnp.where((quadrant & 2) == 2, imag, -imag)
    return real, imag


def residue(first, second):
    return (first * second) & (IMAGE - 1)


def coord_square(coords):
    unit = (coords & (IMAGE - 1)).astype(jnp.float32) / IMAGE - 0.5
    return unit * unit


def times(a, b):
    return a[0] * b[0] - a[1] * b[1], a[0] * b[1] + a[1] * b[0]


def iota(shape, axis):
    return lax.broadcasted_iota(jnp.int32, shape, axis)


def fused_kernel(
    dims,
    image_hbm, wrow_ref, wcol_ref, w_ref, row_off_ref, col_off_ref, band_ref, sub_off_ref, sub_col_ref,
    out_ref,
    left, right, hown, hsend, hgot, band, rtab, coarse, fine, phases,
    part, recv1, sum1, recv2, sum2, recv3, zpart, zrecv1, zsum1, zrecv2, zsum2, zrecv3,
    lsem, isend, irecv, s1, r1, s2, r2, s3, r3, t1, q1, t2, q2, t3, q3,
):
    n_side, n_z, n_sub, facet, sg = dims
    r = lax.axis_index("frow")
    c = lax.axis_index("fcol")
    x, core = c // 2, c % 2
    z, y = r // n_side, r % n_side
    block = sg // (2 * n_side)
    urows = sg // (n_side * n_z)
    up = urows // PARTS
    nv = sg // 2
    partner = (r, c + 1 - 2 * core)
    first = x * (1 - core) + y * core
    second = y * (1 - core) + x * core

    def place(a, b, zz):
        xx = a * (1 - core) + b * core
        yy = b * (1 - core) + a * core
        return (zz * n_side + yy, xx * 2 + core)

    firsts = [(first + d) % n_side for d in range(1, n_side)]
    seconds = [(second + d) % n_side for d in range(1, n_side)]
    zs = [(z + d) % n_z for d in range(1, n_z)]
    peers = (
        [place(first, second, q) for q in zs]
        + [place(a, second, z) for a in firsts]
        + [place(first, b, z) for b in seconds]
        + [partner]
    )
    barrier = pltpu.get_barrier_semaphore()
    for peer in peers:
        pl.semaphore_signal(barrier, inc=1, device_id=peer, device_id_type=MESH)

    loads = [
        pltpu.make_async_copy(
            image_hbm.at[i], left.at[:, i * facet : (i + 1) * facet], lsem.at[i]
        )
        for i in range(2)
    ]
    for load in loads:
        load.start()

    lane = iota((1, facet), 1)
    gcol = col_off_ref[c] + lane
    grow = row_off_ref[r] + lane
    columns = [sub_col_ref[k] for k in range(n_sub)]

    row_id = iota((phases.shape[1], facet), 0)
    angle = jnp.zeros((phases.shape[1], facet), jnp.float32)
    for k in range(n_sub):
        w = w_ref[columns[k]]
        for f, coords in enumerate((gcol, grow)):
            angle = jnp.where(row_id == 2 * k + f, w * coord_square(coords), angle)
    phases[0] = jnp.cos(angle)
    phases[1] = jnp.sin(angle)

    def write_fine(slot, coords):
        q = unit_phasor(residue(coords, iota((ROWS, facet), 0)))
        fine[slot, 0] = q[0]
        fine[slot, 1] = q[1]

    def write_coarse(coords, freqs, gain, row):
        p = times(
            unit_phasor(residue(coords, freqs)),
            (phases[0, row : row + 1, :] * gain, phases[1, row : row + 1, :] * gain),
        )
        coarse[0] = p[0]
        coarse[1] = p[1]

    def entries(slot, h):
        re, im = times(
            (coarse[0, pl.ds(h, 1), :], coarse[1, pl.ds(h, 1), :]), (fine[slot, 0], fine[slot, 1])
        )
        return re.astype(jnp.bfloat16), im.astype(jnp.bfloat16)

    def build_columns(k):
        index = iota((sg // ROWS, facet), 0) * ROWS
        owner = (core + index // nv) % 2
        inner = index % nv
        v = block * (2 * (inner // block) + owner) + inner % block
        write_coarse(gcol, band_ref[columns[k]] + v, wcol_ref[...], 2 * k)
        for side in range(2):

            def body(h, carry, side=side):
                re, im = entries(0, side * (nv // ROWS) + h)
                top = pl.ds(pl.multiple_of(h * ROWS, ROWS), ROWS)
                low = pl.ds(pl.multiple_of(nv + h * ROWS, ROWS), ROWS)
                right[side, k, top, :facet] = re
                right[side, k, top, facet:] = -im
                right[side, k, low, :facet] = im
                right[side, k, low, facet:] = re
                return carry

            lax.fori_loop(0, nv // ROWS, body, 0)

    def build_rows(k):
        index = iota((sg // ROWS, facet), 0) * ROWS
        inner = index % (sg // PARTS)
        per = up * n_z
        u = (
            urows * (n_side * (inner % per // up) + inner // per)
            + up * (index // (sg // PARTS))
            + index % up
        )
        write_coarse(grow, sub_off_ref[k] + u, wrow_ref[...] * scale, 2 * k + 1)

        def body(h, carry):
            re, im = entries(1, h)
            at = pl.ds(pl.multiple_of(h * ROWS, ROWS), ROWS)
            rtab[k, 0, at, :facet] = re
            rtab[k, 0, at, facet:] = -im
            rtab[k, 1, at, :facet] = im
            rtab[k, 1, at, facet:] = re
            return carry

        lax.fori_loop(0, sg // ROWS, body, 0)

    scale = 1.0 / math.sqrt(facet * lax.axis_size("fcol")) / math.sqrt(facet * lax.axis_size("frow"))

    def remote(src, dst, a, b, peer):
        return pltpu.make_async_remote_copy(
            src_ref=src, dst_ref=dst, send_sem=a, recv_sem=b, device_id=peer, device_id_type=MESH
        )

    def contract(side, k):
        return lax.dot_general(
            left[...], right[side, k], (((1,), (1,)), ((), ())), preferred_element_type=jnp.float32
        )

    def advance(group, own, arrived):
        for copy in group:
            copy.wait_recv()
        total = own
        for d in range(len(group)):
            total = total + arrived[d]
        return total

    def launch(group):
        for copy in group:
            copy.start()
        return group

    n_chunk = 2 * n_sub * PARTS
    where = [(k, half, p) for k in range(n_sub) for half in range(2) for p in range(PARTS)]
    rows = up * n_z
    span = sg // PARTS
    swaps, copies1, copies2, copies3, zcopies = [], [], [], [], []

    def emit(ch):
        k, half, p = where[ch]
        value = jnp.dot(
            rtab[k, half, p * span : (p + 1) * span, :],
            band[k],
            preferred_element_type=jnp.float32,
        )
        for yb in range(n_side):
            for xb in range(n_side):
                a = xb * (1 - core) + yb * core
                b = yb * (1 - core) + xb * core
                tile = value[yb * rows : (yb + 1) * rows, xb * block : (xb + 1) * block]
                if ch == 0:
                    for zz in range(n_z):
                        zpart[zz, a, b] = tile[zz * up : (zz + 1) * up]
                else:
                    part[ch, a, b] = tile
        if ch == 0:
            group = [
                remote(zpart.at[q], zrecv1.at[d], t1.at[d], q1.at[d], place(first, second, q))
                for d, q in enumerate(zs)
            ]
            zcopies.append(launch(group))
        else:
            group = [
                remote(part.at[ch, a], recv1.at[ch, d], s1.at[ch, d], r1.at[ch, d], place(a, second, z))
                for d, a in enumerate(firsts)
            ]
            copies1.append(launch(group))

    def finish_second():
        done = len(copies3) + 1
        total = advance(copies2[done - 1], sum1[done, second], recv2.at[done])
        sum2[done] = total.reshape(n_z, up, block)
        group = [
            remote(sum2.at[done, q], recv3.at[done, d], s3.at[done, d], r3.at[done, d], place(first, second, q))
            for d, q in enumerate(zs)
        ]
        copies3.append(launch(group))

    def pump():
        ch = len(copies2) + 1
        sum1[ch] = advance(copies1[ch - 1], part[ch, first], recv1.at[ch])
        group = [
            remote(sum1.at[ch, b], recv2.at[ch, d], s2.at[ch, d], r2.at[ch, d], place(first, b, z))
            for d, b in enumerate(seconds)
        ]
        copies2.append(launch(group))
        if ch == n_chunk // 2:
            zsum1[...] = advance(zcopies[0], zpart[z], zrecv1)
            group = [
                remote(zsum1.at[a], zrecv2.at[d], t2.at[d], q2.at[d], place(a, second, z))
                for d, a in enumerate(firsts)
            ]
            zcopies.append(launch(group))
        if ch >= 2:
            finish_second()

    write_fine(0, gcol)
    for k in range(n_sub):
        build_columns(k)
        if k == 0:
            for load in loads:
                load.wait()
        hsend[k] = contract(1, k)
        if k == 0:
            pl.semaphore_wait(barrier, len(peers))
        swap = remote(hsend.at[k], hgot.at[k], isend.at[k], irecv.at[k], partner)
        swap.start()
        swaps.append(swap)
        hown[k] = contract(0, k)
        if k == 0:
            write_fine(1, grow)
        else:
            pump()
        build_rows(k)
        swap.wait_recv()
        for i in range(2):
            at = slice(i * nv, (i + 1) * nv)
            band[k, i * facet : (i + 1) * facet, :] = (hown[k, :, at] + hgot[k, :, at]).astype(
                jnp.bfloat16
            )
        for ch in range(2 * PARTS * k, 2 * PARTS * (k + 1)):
            emit(ch)
            if k > 0 and ch == 2 * PARTS * k + 1:
                pump()
    while len(copies2) < n_chunk - 1:
        pump()
    finish_second()
    zsum2[...] = advance(zcopies[1], zsum1[first], zrecv2)
    zcopies.append(
        launch(
            [
                remote(zsum2.at[b], zrecv3.at[d], t3.at[d], q3.at[d], place(first, b, z))
                for d, b in enumerate(seconds)
            ]
        )
    )
    for ch, (k, half, p) in enumerate(where):
        if ch > 0:
            total = advance(copies3[ch - 1], sum2[ch, z], recv3.at[ch])
            out_ref[k, half, p * up : (p + 1) * up, :] = total
    out_ref[0, 0, :up, :] = advance(zcopies[2], zsum2[second], zrecv3)
    for swap in swaps:
        swap.wait_send()
    for group in copies1 + copies2 + copies3 + zcopies:
        for copy in group:
            copy.wait_send()


def fused_local(n_side, n_z, image, window_rows, window_cols, *scalars):
    facet = image.shape[1]
    n_sub = scalars[4].shape[0]
    n_chunk = 2 * n_sub * PARTS
    block = SG // (2 * n_side)
    urows = SG // (n_side * n_z)
    up = urows // PARTS
    rows = up * n_z
    f32, b16 = jnp.float32, jnp.bfloat16
    vmem = pl.BlockSpec(memory_space=pltpu.VMEM)
    smem = pl.BlockSpec(memory_space=pltpu.SMEM)
    dma = pltpu.SemaphoreType.DMA
    return pl.pallas_call(
        functools.partial(fused_kernel, (n_side, n_z, n_sub, facet, SG)),
        out_shape=jax.ShapeDtypeStruct((n_sub, 2, urows, block), f32),
        in_specs=[pl.BlockSpec(memory_space=pl.ANY)] + [vmem] * 2 + [smem] * 6,
        out_specs=vmem,
        scratch_shapes=[
            pltpu.VMEM((facet, 2 * facet), b16),
            pltpu.VMEM((2, n_sub, SG, 2 * facet), b16),
            pltpu.VMEM((n_sub, facet, SG), f32),
            pltpu.VMEM((n_sub, facet, SG), f32),
            pltpu.VMEM((n_sub, facet, SG), f32),
            pltpu.VMEM((n_sub, 2 * facet, SG // 2), b16),
            pltpu.VMEM((n_sub, 2, SG, 2 * facet), b16),
            pltpu.VMEM((2, SG // ROWS, facet), f32),
            pltpu.VMEM((2, 2, ROWS, facet), f32),
            pltpu.VMEM((2, -(-2 * n_sub // 8) * 8, facet), f32),
            pltpu.VMEM((n_chunk, n_side, n_side, rows, block), f32),
            pltpu.VMEM((n_chunk, n_side - 1, n_side, rows, block), f32),
            pltpu.VMEM((n_chunk, n_side, rows, block), f32),
            pltpu.VMEM((n_chunk, n_side - 1, rows, block), f32),
            pltpu.VMEM((n_chunk, n_z, up, block), f32),
            pltpu.VMEM((n_chunk, n_z - 1, up, block), f32),
            pltpu.VMEM((n_z, n_side, n_side, up, block), f32),
            pltpu.VMEM((n_z - 1, n_side, n_side, up, block), f32),
            pltpu.VMEM((n_side, n_side, up, block), f32),
            pltpu.VMEM((n_side - 1, n_side, up, block), f32),
            pltpu.VMEM((n_side, up, block), f32),
            pltpu.VMEM((n_side - 1, up, block), f32),
            dma((2,)),
            dma((n_sub,)),
            dma((n_sub,)),
            dma((n_chunk, n_side - 1)),
            dma((n_chunk, n_side - 1)),
            dma((n_chunk, n_side - 1)),
            dma((n_chunk, n_side - 1)),
            dma((n_chunk, n_z - 1)),
            dma((n_chunk, n_z - 1)),
            dma((n_z - 1,)),
            dma((n_z - 1,)),
            dma((n_side - 1,)),
            dma((n_side - 1,)),
            dma((n_side - 1,)),
            dma((n_side - 1,)),
        ],
        compiler_params=pltpu.CompilerParams(
            collective_id=0, has_side_effects=True, vmem_limit_bytes=56 << 20
        ),
    )(image, window_rows.reshape(1, -1), window_cols.reshape(1, -1), *scalars)


def solution(mesh):
    n_side = mesh.shape["fcol"] // 2
    n_z = mesh.shape["frow"] // n_side
    tiled = (
        n_side >= 2
        and n_z >= 2
        and mesh.shape["fcol"] == 2 * n_side
        and mesh.shape["frow"] == n_z * n_side
        and SG % (2 * n_side * 128) == 0
        and SG % (n_side * n_z * ROWS * PARTS) == 0
    )

    def local(image, *rest):
        if tiled and image.shape[1] == image.shape[2] and image.shape[1] % 128 == 0:
            return fused_local(n_side, n_z, image, *rest)
        return general_local(image, *rest)

    placed = (P(None, "frow", "fcol"), P("frow"), P("fcol"), P(), P(), P(), P(), P(), P())
    return jax.shard_map(
        local, mesh=mesh, in_specs=placed, out_specs=P(None, None, "frow", "fcol"), check_vma=False
    )
```

```python
import functools
import math

import jax
import jax.numpy as jnp
from jax import lax
from jax.experimental import pallas as pl
from jax.experimental.pallas import tpu as pltpu
from jax.sharding import PartitionSpec as P

SG = 512
IMAGE = 65536


def phase_index(first, second):
    high = first * (second // 256) % 256 * 256
    return (high + first * (second % 256)) % 65536


def dft_table(coords, freqs):
    angle = phase_index(coords, freqs).astype(jnp.float32) * (2.0 * math.pi / IMAGE)
    return (jnp.cos(angle).astype(jnp.bfloat16), (-jnp.sin(angle)).astype(jnp.bfloat16))


def coord_unit(coords):
    return (coords % IMAGE).astype(jnp.float32) / IMAGE - 0.5


def block_table(table_re, table_im):
    upper = jnp.concatenate([table_re, table_im], axis=1)
    lower = jnp.concatenate([-table_im, table_re], axis=1)
    return jnp.concatenate([upper, lower], axis=0)


def general_local(
    image,
    window_rows,
    window_cols,
    w_terms,
    facet_row_offset,
    facet_col_offset,
    band_offset,
    sub_row_offset,
    sub_column,
):
    facet = image.shape[1]
    column_count = band_offset.shape[0]
    sub_count = sub_row_offset.shape[0]
    frow_index = lax.axis_index("frow")
    fcol_index = lax.axis_index("fcol")
    freq_base = jnp.arange(SG, dtype=jnp.int32)
    gcol = facet_col_offset[fcol_index] + jnp.arange(image.shape[2], dtype=jnp.int32)
    mcoord = coord_unit(gcol)
    row_base = facet_row_offset[frow_index]
    row_ids = row_base + jnp.arange(facet, dtype=jnp.int32)
    radius = coord_unit(row_ids)[:, None] ** 2 + mcoord[None, :] ** 2
    scale = window_rows[:, None] * window_cols[None, :]
    first = image[0].astype(jnp.float32) * scale
    second = image[1].astype(jnp.float32) * scale
    prepared = []
    for column in range(column_count):
        angle = w_terms[column] * radius
        cosine = jnp.cos(angle)
        sine = jnp.sin(angle)
        prep_re = (first * cosine - second * sine).astype(jnp.bfloat16)
        prep_im = (first * sine + second * cosine).astype(jnp.bfloat16)
        prepared.append(jnp.concatenate([prep_re, prep_im], axis=1))
    band_dev = SG // lax.axis_size("fcol")
    freqs = jnp.arange(band_dev * lax.axis_size("fcol"), dtype=jnp.int32)
    outputs = []
    for column in range(column_count):
        table_re, table_im = dft_table(gcol[:, None], band_offset[column] + freqs[None, :])
        whole_table = block_table(table_re, table_im)
        product = lax.dot_general(
            whole_table,
            prepared[column],
            (((0,), (1,)), ((), ())),
            preferred_element_type=jnp.float32,
        )
        outputs.append(
            product.reshape(2, band_dev * lax.axis_size("fcol"), facet).transpose(1, 0, 2)
        )
    summed = lax.psum_scatter(jnp.stack(outputs, axis=1), "fcol", scatter_dimension=0, tiled=True)
    banded = (summed / math.sqrt(facet * lax.axis_size("fcol"))).astype(jnp.bfloat16)
    chosen = jnp.take(banded, sub_column, axis=1)
    right_side = chosen.transpose(1, 2, 3, 0).reshape(sub_count, 2 * facet, band_dev)
    table_re, table_im = dft_table(
        row_ids[None, :, None], sub_row_offset[:, None, None] + freq_base[None, None, :]
    )
    left_real = jnp.concatenate([table_re, -table_im], axis=1)
    left_imag = jnp.concatenate([table_im, table_re], axis=1)
    left_side = jnp.stack([left_real, left_imag], axis=2)
    term = jnp.einsum("kxcu,kxv->kcuv", left_side, right_side, preferred_element_type=jnp.float32)
    term = term * (1.0 / math.sqrt(facet * lax.axis_size("frow")))
    return lax.psum_scatter(term, "frow", scatter_dimension=2, tiled=True)


MESH = pl.DeviceIdType.MESH
ROWS = 16
PARTS = 2


def unit_phasor(index):
    quadrant = (index + IMAGE // 8) >> 14
    t = (index - (quadrant << 14)).astype(jnp.float32) * (2.0 * math.pi / IMAGE)
    s = t * t
    sine = t * (1.0 + s * (-1 / 6 + s * (1 / 120 + s * (-1 / 5040 + s * (1 / 362880)))))
    cosine = 1.0 + s * (
        -1 / 2 + s * (1 / 24 + s * (-1 / 720 + s * (1 / 40320 + s * (-1 / 3628800))))
    )
    odd = (quadrant & 1) == 1
    real = jnp.where(odd, sine, cosine)
    imag = jnp.where(odd, cosine, sine)
    real = jnp.where(((quadrant + 1) & 2) == 2, -real, real)
    imag = jnp.where((quadrant & 2) == 2, imag, -imag)
    return real, imag


def residue(first, second):
    return (first * second) & (IMAGE - 1)


def coord_square(coords):
    unit = (coords & (IMAGE - 1)).astype(jnp.float32) / IMAGE - 0.5
    return unit * unit


def times(a, b):
    return a[0] * b[0] - a[1] * b[1], a[0] * b[1] + a[1] * b[0]


def iota(shape, axis):
    return lax.broadcasted_iota(jnp.int32, shape, axis)


def fused_kernel(
    dims,
    image_hbm, wrow_ref, wcol_ref, w_ref, row_off_ref, col_off_ref, band_ref, sub_off_ref, sub_col_ref,
    out_ref,
    left, right, hown, hsend, hgot, band, rtab, coarse, fine, phases,
    part, recv1, sum1, recv2, sum2, recv3, zpart, zrecv1, zsum1, zrecv2, zsum2, zrecv3,
    lsem, isend, irecv, s1, r1, s2, r2, s3, r3, t1, q1, t2, q2, t3, q3,
):
    n_side, n_z, n_sub, facet, sg = dims
    r = lax.axis_index("frow")
    c = lax.axis_index("fcol")
    x, core = c // 2, c % 2
    z, y = r // n_side, r % n_side
    block = sg // (2 * n_side)
    urows = sg // (n_side * n_z)
    up = urows // PARTS
    nv = sg // 2
    partner = (r, c + 1 - 2 * core)
    first = x * (1 - core) + y * core
    second = y * (1 - core) + x * core

    def place(a, b, zz):
        xx = a * (1 - core) + b * core
        yy = b * (1 - core) + a * core
        return (zz * n_side + yy, xx * 2 + core)

    firsts = [(first + d) % n_side for d in range(1, n_side)]
    seconds = [(second + d) % n_side for d in range(1, n_side)]
    zs = [(z + d) % n_z for d in range(1, n_z)]
    peers = (
        [place(first, second, q) for q in zs]
        + [place(a, second, z) for a in firsts]
        + [place(first, b, z) for b in seconds]
        + [partner]
    )
    barrier = pltpu.get_barrier_semaphore()
    for peer in peers:
        pl.semaphore_signal(barrier, inc=1, device_id=peer, device_id_type=MESH)

    loads = [
        pltpu.make_async_copy(
            image_hbm.at[i], left.at[:, i * facet : (i + 1) * facet], lsem.at[i]
        )
        for i in range(2)
    ]
    for load in loads:
        load.start()

    lane = iota((1, facet), 1)
    gcol = col_off_ref[c] + lane
    grow = row_off_ref[r] + lane
    columns = [sub_col_ref[k] for k in range(n_sub)]

    row_id = iota((phases.shape[1], facet), 0)
    angle = jnp.zeros((phases.shape[1], facet), jnp.float32)
    for k in range(n_sub):
        w = w_ref[columns[k]]
        for f, coords in enumerate((gcol, grow)):
            angle = jnp.where(row_id == 2 * k + f, w * coord_square(coords), angle)
    phases[0] = jnp.cos(angle)
    phases[1] = jnp.sin(angle)

    def write_fine(slot, coords):
        q = unit_phasor(residue(coords, iota((ROWS, facet), 0)))
        fine[slot, 0] = q[0]
        fine[slot, 1] = q[1]

    def write_coarse(coords, freqs, gain, row):
        p = times(
            unit_phasor(residue(coords, freqs)),
            (phases[0, row : row + 1, :] * gain, phases[1, row : row + 1, :] * gain),
        )
        coarse[0] = p[0]
        coarse[1] = p[1]

    def entries(slot, h):
        re, im = times(
            (coarse[0, pl.ds(h, 1), :], coarse[1, pl.ds(h, 1), :]), (fine[slot, 0], fine[slot, 1])
        )
        return re.astype(jnp.bfloat16), im.astype(jnp.bfloat16)

    def column_phases(k):
        index = iota((sg // ROWS, facet), 0) * ROWS
        owner = (core + index // nv) % 2
        inner = index % nv
        v = block * (2 * (inner // block) + owner) + inner % block
        write_coarse(gcol, band_ref[columns[k]] + v, wcol_ref[...], 2 * k)

    def build_columns(side, k):
        def body(h, carry):
            re, im = entries(0, side * (nv // ROWS) + h)
            top = pl.ds(pl.multiple_of(h * ROWS, ROWS), ROWS)
            low = pl.ds(pl.multiple_of(nv + h * ROWS, ROWS), ROWS)
            right[side, k, top, :facet] = re
            right[side, k, top, facet:] = -im
            right[side, k, low, :facet] = im
            right[side, k, low, facet:] = re
            return carry

        lax.fori_loop(0, nv // ROWS, body, 0)

    def build_rows(k):
        index = iota((sg // ROWS, facet), 0) * ROWS
        inner = index % (sg // PARTS)
        per = up * n_z
        u = (
            urows * (n_side * (inner % per // up) + inner // per)
            + up * (index // (sg // PARTS))
            + index % up
        )
        write_coarse(grow, sub_off_ref[k] + u, wrow_ref[...] * scale, 2 * k + 1)

        def body(h, carry):
            re, im = entries(1, h)
            at = pl.ds(pl.multiple_of(h * ROWS, ROWS), ROWS)
            rtab[k, 0, at, :facet] = re
            rtab[k, 0, at, facet:] = -im
            rtab[k, 1, at, :facet] = im
            rtab[k, 1, at, facet:] = re
            return carry

        lax.fori_loop(0, sg // ROWS, body, 0)

    scale = 1.0 / math.sqrt(facet * lax.axis_size("fcol")) / math.sqrt(facet * lax.axis_size("frow"))

    def remote(src, dst, a, b, peer):
        return pltpu.make_async_remote_copy(
            src_ref=src, dst_ref=dst, send_sem=a, recv_sem=b, device_id=peer, device_id_type=MESH
        )

    def contract(side, k):
        return lax.dot_general(
            left[...], right[side, k], (((1,), (1,)), ((), ())), preferred_element_type=jnp.float32
        )

    def advance(group, own, arrived):
        for copy in group:
            copy.wait_recv()
        total = own
        for d in range(len(group)):
            total = total + arrived[d]
        return total

    def launch(group):
        for copy in group:
            copy.start()
        return group

    n_chunk = 2 * n_sub * PARTS
    where = [(k, half, p) for k in range(n_sub) for half in range(2) for p in range(PARTS)]
    rows = up * n_z
    span = sg // PARTS
    swaps, copies1, copies2, copies3, zcopies = [], [], [], [], []

    def emit(ch):
        k, half, p = where[ch]
        value = jnp.dot(
            rtab[k, half, p * span : (p + 1) * span, :],
            band[k],
            preferred_element_type=jnp.float32,
        )
        for yb in range(n_side):
            for xb in range(n_side):
                a = xb * (1 - core) + yb * core
                b = yb * (1 - core) + xb * core
                tile = value[yb * rows : (yb + 1) * rows, xb * block : (xb + 1) * block]
                if ch == 0:
                    for zz in range(n_z):
                        zpart[zz, a, b] = tile[zz * up : (zz + 1) * up]
                else:
                    part[ch, a, b] = tile
        if ch == 0:
            group = [
                remote(zpart.at[q], zrecv1.at[d], t1.at[d], q1.at[d], place(first, second, q))
                for d, q in enumerate(zs)
            ]
            zcopies.append(launch(group))
        else:
            group = [
                remote(part.at[ch, a], recv1.at[ch, d], s1.at[ch, d], r1.at[ch, d], place(a, second, z))
                for d, a in enumerate(firsts)
            ]
            copies1.append(launch(group))

    def finish_second():
        done = len(copies3) + 1
        total = advance(copies2[done - 1], sum1[done, second], recv2.at[done])
        sum2[done] = total.reshape(n_z, up, block)
        group = [
            remote(sum2.at[done, q], recv3.at[done, d], s3.at[done, d], r3.at[done, d], place(first, second, q))
            for d, q in enumerate(zs)
        ]
        copies3.append(launch(group))

    def pump():
        ch = len(copies2) + 1
        sum1[ch] = advance(copies1[ch - 1], part[ch, first], recv1.at[ch])
        group = [
            remote(sum1.at[ch, b], recv2.at[ch, d], s2.at[ch, d], r2.at[ch, d], place(first, b, z))
            for d, b in enumerate(seconds)
        ]
        copies2.append(launch(group))
        if ch == n_chunk // 2:
            zsum1[...] = advance(zcopies[0], zpart[z], zrecv1)
            group = [
                remote(zsum1.at[a], zrecv2.at[d], t2.at[d], q2.at[d], place(a, second, z))
                for d, a in enumerate(firsts)
            ]
            zcopies.append(launch(group))
        if ch >= 2:
            finish_second()

    write_fine(0, gcol)
    for k in range(n_sub):
        column_phases(k)
        build_columns(1, k)
        if k == 0:
            for load in loads:
                load.wait()
        hsend[k] = contract(1, k)
        if k == 0:
            pl.semaphore_wait(barrier, len(peers))
        swap = remote(hsend.at[k], hgot.at[k], isend.at[k], irecv.at[k], partner)
        swap.start()
        swaps.append(swap)
        build_columns(0, k)
        hown[k] = contract(0, k)
        if k == 0:
            write_fine(1, grow)
        else:
            pump()
        build_rows(k)
        swap.wait_recv()
        for i in range(2):
            at = slice(i * nv, (i + 1) * nv)
            band[k, i * facet : (i + 1) * facet, :] = (hown[k, :, at] + hgot[k, :, at]).astype(
                jnp.bfloat16
            )
        for ch in range(2 * PARTS * k, 2 * PARTS * (k + 1)):
            emit(ch)
            if k > 0 and ch == 2 * PARTS * k + 1:
                pump()
    while len(copies2) < n_chunk - 1:
        pump()
    finish_second()
    zsum2[...] = advance(zcopies[1], zsum1[first], zrecv2)
    zcopies.append(
        launch(
            [
                remote(zsum2.at[b], zrecv3.at[d], t3.at[d], q3.at[d], place(first, b, z))
                for d, b in enumerate(seconds)
            ]
        )
    )
    for ch, (k, half, p) in enumerate(where):
        if ch > 0:
            total = advance(copies3[ch - 1], sum2[ch, z], recv3.at[ch])
            out_ref[k, half, p * up : (p + 1) * up, :] = total
    out_ref[0, 0, :up, :] = advance(zcopies[2], zsum2[second], zrecv3)
    for swap in swaps:
        swap.wait_send()
    for group in copies1 + copies2 + copies3 + zcopies:
        for copy in group:
            copy.wait_send()


def fused_local(n_side, n_z, image, window_rows, window_cols, *scalars):
    facet = image.shape[1]
    n_sub = scalars[4].shape[0]
    n_chunk = 2 * n_sub * PARTS
    block = SG // (2 * n_side)
    urows = SG // (n_side * n_z)
    up = urows // PARTS
    rows = up * n_z
    f32, b16 = jnp.float32, jnp.bfloat16
    vmem = pl.BlockSpec(memory_space=pltpu.VMEM)
    smem = pl.BlockSpec(memory_space=pltpu.SMEM)
    dma = pltpu.SemaphoreType.DMA
    return pl.pallas_call(
        functools.partial(fused_kernel, (n_side, n_z, n_sub, facet, SG)),
        out_shape=jax.ShapeDtypeStruct((n_sub, 2, urows, block), f32),
        in_specs=[pl.BlockSpec(memory_space=pl.ANY)] + [vmem] * 2 + [smem] * 6,
        out_specs=vmem,
        scratch_shapes=[
            pltpu.VMEM((facet, 2 * facet), b16),
            pltpu.VMEM((2, n_sub, SG, 2 * facet), b16),
            pltpu.VMEM((n_sub, facet, SG), f32),
            pltpu.VMEM((n_sub, facet, SG), f32),
            pltpu.VMEM((n_sub, facet, SG), f32),
            pltpu.VMEM((n_sub, 2 * facet, SG // 2), b16),
            pltpu.VMEM((n_sub, 2, SG, 2 * facet), b16),
            pltpu.VMEM((2, SG // ROWS, facet), f32),
            pltpu.VMEM((2, 2, ROWS, facet), f32),
            pltpu.VMEM((2, -(-2 * n_sub // 8) * 8, facet), f32),
            pltpu.VMEM((n_chunk, n_side, n_side, rows, block), f32),
            pltpu.VMEM((n_chunk, n_side - 1, n_side, rows, block), f32),
            pltpu.VMEM((n_chunk, n_side, rows, block), f32),
            pltpu.VMEM((n_chunk, n_side - 1, rows, block), f32),
            pltpu.VMEM((n_chunk, n_z, up, block), f32),
            pltpu.VMEM((n_chunk, n_z - 1, up, block), f32),
            pltpu.VMEM((n_z, n_side, n_side, up, block), f32),
            pltpu.VMEM((n_z - 1, n_side, n_side, up, block), f32),
            pltpu.VMEM((n_side, n_side, up, block), f32),
            pltpu.VMEM((n_side - 1, n_side, up, block), f32),
            pltpu.VMEM((n_side, up, block), f32),
            pltpu.VMEM((n_side - 1, up, block), f32),
            dma((2,)),
            dma((n_sub,)),
            dma((n_sub,)),
            dma((n_chunk, n_side - 1)),
            dma((n_chunk, n_side - 1)),
            dma((n_chunk, n_side - 1)),
            dma((n_chunk, n_side - 1)),
            dma((n_chunk, n_z - 1)),
            dma((n_chunk, n_z - 1)),
            dma((n_z - 1,)),
            dma((n_z - 1,)),
            dma((n_side - 1,)),
            dma((n_side - 1,)),
            dma((n_side - 1,)),
            dma((n_side - 1,)),
        ],
        compiler_params=pltpu.CompilerParams(
            collective_id=0, has_side_effects=True, vmem_limit_bytes=56 << 20
        ),
    )(image, window_rows.reshape(1, -1), window_cols.reshape(1, -1), *scalars)


def solution(mesh):
    n_side = mesh.shape["fcol"] // 2
    n_z = mesh.shape["frow"] // n_side
    tiled = (
        n_side >= 2
        and n_z >= 2
        and mesh.shape["fcol"] == 2 * n_side
        and mesh.shape["frow"] == n_z * n_side
        and SG % (2 * n_side * 128) == 0
        and SG % (n_side * n_z * ROWS * PARTS) == 0
    )

    def local(image, *rest):
        if tiled and image.shape[1] == image.shape[2] and image.shape[1] % 128 == 0:
            return fused_local(n_side, n_z, image, *rest)
        return general_local(image, *rest)

    placed = (P(None, "frow", "fcol"), P("frow"), P("fcol"), P(), P(), P(), P(), P(), P())
    return jax.shard_map(
        local, mesh=mesh, in_specs=placed, out_specs=P(None, None, "frow", "fcol"), check_vma=False
    )
```

```python
import functools
import math

import jax
import jax.numpy as jnp
from jax import lax
from jax.experimental import pallas as pl
from jax.experimental.pallas import tpu as pltpu
from jax.sharding import PartitionSpec as P

SG = 512
IMAGE = 65536


def phase_index(first, second):
    high = first * (second // 256) % 256 * 256
    return (high + first * (second % 256)) % 65536


def dft_table(coords, freqs):
    angle = phase_index(coords, freqs).astype(jnp.float32) * (2.0 * math.pi / IMAGE)
    return (jnp.cos(angle).astype(jnp.bfloat16), (-jnp.sin(angle)).astype(jnp.bfloat16))


def coord_unit(coords):
    return (coords % IMAGE).astype(jnp.float32) / IMAGE - 0.5


def block_table(table_re, table_im):
    upper = jnp.concatenate([table_re, table_im], axis=1)
    lower = jnp.concatenate([-table_im, table_re], axis=1)
    return jnp.concatenate([upper, lower], axis=0)


def general_local(
    image,
    window_rows,
    window_cols,
    w_terms,
    facet_row_offset,
    facet_col_offset,
    band_offset,
    sub_row_offset,
    sub_column,
):
    facet = image.shape[1]
    column_count = band_offset.shape[0]
    sub_count = sub_row_offset.shape[0]
    frow_index = lax.axis_index("frow")
    fcol_index = lax.axis_index("fcol")
    freq_base = jnp.arange(SG, dtype=jnp.int32)
    gcol = facet_col_offset[fcol_index] + jnp.arange(image.shape[2], dtype=jnp.int32)
    mcoord = coord_unit(gcol)
    row_base = facet_row_offset[frow_index]
    row_ids = row_base + jnp.arange(facet, dtype=jnp.int32)
    radius = coord_unit(row_ids)[:, None] ** 2 + mcoord[None, :] ** 2
    scale = window_rows[:, None] * window_cols[None, :]
    first = image[0].astype(jnp.float32) * scale
    second = image[1].astype(jnp.float32) * scale
    prepared = []
    for column in range(column_count):
        angle = w_terms[column] * radius
        cosine = jnp.cos(angle)
        sine = jnp.sin(angle)
        prep_re = (first * cosine - second * sine).astype(jnp.bfloat16)
        prep_im = (first * sine + second * cosine).astype(jnp.bfloat16)
        prepared.append(jnp.concatenate([prep_re, prep_im], axis=1))
    band_dev = SG // lax.axis_size("fcol")
    freqs = jnp.arange(band_dev * lax.axis_size("fcol"), dtype=jnp.int32)
    outputs = []
    for column in range(column_count):
        table_re, table_im = dft_table(gcol[:, None], band_offset[column] + freqs[None, :])
        whole_table = block_table(table_re, table_im)
        product = lax.dot_general(
            whole_table,
            prepared[column],
            (((0,), (1,)), ((), ())),
            preferred_element_type=jnp.float32,
        )
        outputs.append(
            product.reshape(2, band_dev * lax.axis_size("fcol"), facet).transpose(1, 0, 2)
        )
    summed = lax.psum_scatter(jnp.stack(outputs, axis=1), "fcol", scatter_dimension=0, tiled=True)
    banded = (summed / math.sqrt(facet * lax.axis_size("fcol"))).astype(jnp.bfloat16)
    chosen = jnp.take(banded, sub_column, axis=1)
    right_side = chosen.transpose(1, 2, 3, 0).reshape(sub_count, 2 * facet, band_dev)
    table_re, table_im = dft_table(
        row_ids[None, :, None], sub_row_offset[:, None, None] + freq_base[None, None, :]
    )
    left_real = jnp.concatenate([table_re, -table_im], axis=1)
    left_imag = jnp.concatenate([table_im, table_re], axis=1)
    left_side = jnp.stack([left_real, left_imag], axis=2)
    term = jnp.einsum("kxcu,kxv->kcuv", left_side, right_side, preferred_element_type=jnp.float32)
    term = term * (1.0 / math.sqrt(facet * lax.axis_size("frow")))
    return lax.psum_scatter(term, "frow", scatter_dimension=2, tiled=True)


MESH = pl.DeviceIdType.MESH
ROWS = 16
PARTS = 2


def unit_phasor(index):
    quadrant = (index + IMAGE // 8) >> 14
    t = (index - (quadrant << 14)).astype(jnp.float32) * (2.0 * math.pi / IMAGE)
    s = t * t
    sine = t * (1.0 + s * (-1 / 6 + s * (1 / 120 + s * (-1 / 5040 + s * (1 / 362880)))))
    cosine = 1.0 + s * (
        -1 / 2 + s * (1 / 24 + s * (-1 / 720 + s * (1 / 40320 + s * (-1 / 3628800))))
    )
    odd = (quadrant & 1) == 1
    real = jnp.where(odd, sine, cosine)
    imag = jnp.where(odd, cosine, sine)
    real = jnp.where(((quadrant + 1) & 2) == 2, -real, real)
    imag = jnp.where((quadrant & 2) == 2, imag, -imag)
    return real, imag


def residue(first, second):
    return (first * second) & (IMAGE - 1)


def coord_square(coords):
    unit = (coords & (IMAGE - 1)).astype(jnp.float32) / IMAGE - 0.5
    return unit * unit


def times(a, b):
    return a[0] * b[0] - a[1] * b[1], a[0] * b[1] + a[1] * b[0]


def iota(shape, axis):
    return lax.broadcasted_iota(jnp.int32, shape, axis)


def fused_kernel(
    dims,
    image_hbm, wrow_ref, wcol_ref, w_ref, row_off_ref, col_off_ref, band_ref, sub_off_ref, sub_col_ref,
    out_ref,
    left, right, hown, hsend, hgot, band, rtab, coarse, fine, phases,
    part, recv1, sum1, recv2, sum2, recv3, zpart, zrecv1, zsum1, zrecv2, zsum2, zrecv3,
    lsem, isend, irecv, s1, r1, s2, r2, s3, r3, t1, q1, t2, q2, t3, q3,
):
    n_side, n_z, n_sub, facet, sg = dims
    r = lax.axis_index("frow")
    c = lax.axis_index("fcol")
    x, core = c // 2, c % 2
    z, y = r // n_side, r % n_side
    block = sg // (2 * n_side)
    urows = sg // (n_side * n_z)
    up = urows // PARTS
    nv = sg // 2
    partner = (r, c + 1 - 2 * core)
    first = x * (1 - core) + y * core
    second = y * (1 - core) + x * core

    def place(a, b, zz):
        xx = a * (1 - core) + b * core
        yy = b * (1 - core) + a * core
        return (zz * n_side + yy, xx * 2 + core)

    firsts = [(first + d) % n_side for d in range(1, n_side)]
    seconds = [(second + d) % n_side for d in range(1, n_side)]
    zs = [(z + d) % n_z for d in range(1, n_z)]
    peers = (
        [place(first, second, q) for q in zs]
        + [place(a, second, z) for a in firsts]
        + [place(first, b, z) for b in seconds]
        + [partner]
    )
    barrier = pltpu.get_barrier_semaphore()
    for peer in peers:
        pl.semaphore_signal(barrier, inc=1, device_id=peer, device_id_type=MESH)

    loads = [
        pltpu.make_async_copy(
            image_hbm.at[i], left.at[:, i * facet : (i + 1) * facet], lsem.at[i]
        )
        for i in range(2)
    ]
    for load in loads:
        load.start()

    lane = iota((1, facet), 1)
    gcol = col_off_ref[c] + lane
    grow = row_off_ref[r] + lane
    columns = [sub_col_ref[k] for k in range(n_sub)]

    row_id = iota((phases.shape[1], facet), 0)
    angle = jnp.zeros((phases.shape[1], facet), jnp.float32)
    for k in range(n_sub):
        w = w_ref[columns[k]]
        for f, coords in enumerate((gcol, grow)):
            angle = jnp.where(row_id == 2 * k + f, w * coord_square(coords), angle)
    phases[0] = jnp.cos(angle)
    phases[1] = jnp.sin(angle)

    def write_fine(slot, coords):
        q = unit_phasor(residue(coords, iota((ROWS, facet), 0)))
        fine[slot, 0] = q[0]
        fine[slot, 1] = q[1]

    def write_coarse(coords, freqs, gain, row):
        p = times(
            unit_phasor(residue(coords, freqs)),
            (phases[0, row : row + 1, :] * gain, phases[1, row : row + 1, :] * gain),
        )
        coarse[0] = p[0]
        coarse[1] = p[1]

    def entries(slot, h):
        re, im = times(
            (coarse[0, pl.ds(h, 1), :], coarse[1, pl.ds(h, 1), :]), (fine[slot, 0], fine[slot, 1])
        )
        return re.astype(jnp.bfloat16), im.astype(jnp.bfloat16)

    def column_phases(k):
        index = iota((sg // ROWS, facet), 0) * ROWS
        owner = (core + index // nv) % 2
        inner = index % nv
        v = block * (2 * (inner // block) + owner) + inner % block
        write_coarse(gcol, band_ref[columns[k]] + v, wcol_ref[...], 2 * k)

    def build_columns(side, k):
        def body(h, carry):
            re, im = entries(0, side * (nv // ROWS) + h)
            top = pl.ds(pl.multiple_of(h * ROWS, ROWS), ROWS)
            low = pl.ds(pl.multiple_of(nv + h * ROWS, ROWS), ROWS)
            right[side, k, top, :facet] = re
            right[side, k, top, facet:] = -im
            right[side, k, low, :facet] = im
            right[side, k, low, facet:] = re
            return carry

        lax.fori_loop(0, nv // ROWS, body, 0)

    def build_rows(k):
        index = iota((sg // ROWS, facet), 0) * ROWS
        inner = index % (sg // PARTS)
        per = up * n_z
        u = (
            urows * (n_side * (inner % per // up) + inner // per)
            + up * (index // (sg // PARTS))
            + index % up
        )
        write_coarse(grow, sub_off_ref[k] + u, wrow_ref[...] * scale, 2 * k + 1)

        def body(h, carry):
            re, im = entries(1, h)
            at = pl.ds(pl.multiple_of(h * ROWS, ROWS), ROWS)
            rtab[k, 0, at, :facet] = re
            rtab[k, 0, at, facet:] = -im
            rtab[k, 1, at, :facet] = im
            rtab[k, 1, at, facet:] = re
            return carry

        lax.fori_loop(0, sg // ROWS, body, 0)

    scale = 1.0 / math.sqrt(facet * lax.axis_size("fcol")) / math.sqrt(facet * lax.axis_size("frow"))

    def remote(src, dst, a, b, peer):
        return pltpu.make_async_remote_copy(
            src_ref=src, dst_ref=dst, send_sem=a, recv_sem=b, device_id=peer, device_id_type=MESH
        )

    def contract(side, k):
        return lax.dot_general(
            left[...], right[side, k], (((1,), (1,)), ((), ())), preferred_element_type=jnp.float32
        )

    def advance(group, own, arrived):
        for copy in group:
            copy.wait_recv()
        total = own
        for d in range(len(group)):
            total = total + arrived[d]
        return total

    def launch(group):
        for copy in group:
            copy.start()
        return group

    n_chunk = 2 * n_sub * PARTS
    where = [(k, half, p) for k in range(n_sub) for half in range(2) for p in range(PARTS)]
    rows = up * n_z
    span = sg // PARTS
    swaps, copies1, copies2, copies3, zcopies = [], [], [], [], []

    def emit(ch):
        k, half, p = where[ch]
        value = jnp.dot(
            rtab[k, half, p * span : (p + 1) * span, :],
            band[k],
            preferred_element_type=jnp.float32,
        )
        for yb in range(n_side):
            for xb in range(n_side):
                a = xb * (1 - core) + yb * core
                b = yb * (1 - core) + xb * core
                tile = value[yb * rows : (yb + 1) * rows, xb * block : (xb + 1) * block]
                if ch == 0:
                    for zz in range(n_z):
                        zpart[zz, a, b] = tile[zz * up : (zz + 1) * up]
                else:
                    part[ch, a, b] = tile
        if ch == 0:
            group = [
                remote(zpart.at[q], zrecv1.at[d], t1.at[d], q1.at[d], place(first, second, q))
                for d, q in enumerate(zs)
            ]
            zcopies.append(launch(group))
        else:
            group = [
                remote(part.at[ch, a], recv1.at[ch, d], s1.at[ch, d], r1.at[ch, d], place(a, second, z))
                for d, a in enumerate(firsts)
            ]
            copies1.append(launch(group))

    def finish_second():
        done = len(copies3) + 1
        total = advance(copies2[done - 1], sum1[done, second], recv2.at[done])
        sum2[done] = total.reshape(n_z, up, block)
        group = [
            remote(sum2.at[done, q], recv3.at[done, d], s3.at[done, d], r3.at[done, d], place(first, second, q))
            for d, q in enumerate(zs)
        ]
        copies3.append(launch(group))

    def pump():
        ch = len(copies2) + 1
        sum1[ch] = advance(copies1[ch - 1], part[ch, first], recv1.at[ch])
        group = [
            remote(sum1.at[ch, b], recv2.at[ch, d], s2.at[ch, d], r2.at[ch, d], place(first, b, z))
            for d, b in enumerate(seconds)
        ]
        copies2.append(launch(group))
        if ch == n_chunk // 2:
            zsum1[...] = advance(zcopies[0], zpart[z], zrecv1)
            group = [
                remote(zsum1.at[a], zrecv2.at[d], t2.at[d], q2.at[d], place(a, second, z))
                for d, a in enumerate(firsts)
            ]
            zcopies.append(launch(group))
        if ch >= 2:
            finish_second()

    write_fine(0, gcol)
    for k in range(n_sub):
        column_phases(k)
        build_columns(1, k)
        if k == 0:
            for load in loads:
                load.wait()
        hsend[k] = contract(1, k)
        if k == 0:
            pl.semaphore_wait(barrier, len(peers))
        swap = remote(hsend.at[k], hgot.at[k], isend.at[k], irecv.at[k], partner)
        swap.start()
        swaps.append(swap)
        build_columns(0, k)
        hown[k] = contract(0, k)
        if k == 0:
            write_fine(1, grow)
        else:
            pump()
        build_rows(k)
        swap.wait_recv()
        for i in range(2):
            at = slice(i * nv, (i + 1) * nv)
            band[k, i * facet : (i + 1) * facet, :] = (hown[k, :, at] + hgot[k, :, at]).astype(
                jnp.bfloat16
            )
        for ch in range(2 * PARTS * k, 2 * PARTS * (k + 1)):
            emit(ch)
            if k > 0 and ch >= 2 * PARTS * k + 1:
                pump()
    while len(copies2) < n_chunk - 1:
        pump()
    finish_second()
    zsum2[...] = advance(zcopies[1], zsum1[first], zrecv2)
    zcopies.append(
        launch(
            [
                remote(zsum2.at[b], zrecv3.at[d], t3.at[d], q3.at[d], place(first, b, z))
                for d, b in enumerate(seconds)
            ]
        )
    )
    for ch, (k, half, p) in enumerate(where):
        if ch > 0:
            total = advance(copies3[ch - 1], sum2[ch, z], recv3.at[ch])
            out_ref[k, half, p * up : (p + 1) * up, :] = total
    out_ref[0, 0, :up, :] = advance(zcopies[2], zsum2[second], zrecv3)
    for swap in swaps:
        swap.wait_send()
    for group in copies1 + copies2 + copies3 + zcopies:
        for copy in group:
            copy.wait_send()


def fused_local(n_side, n_z, image, window_rows, window_cols, *scalars):
    facet = image.shape[1]
    n_sub = scalars[4].shape[0]
    n_chunk = 2 * n_sub * PARTS
    block = SG // (2 * n_side)
    urows = SG // (n_side * n_z)
    up = urows // PARTS
    rows = up * n_z
    f32, b16 = jnp.float32, jnp.bfloat16
    vmem = pl.BlockSpec(memory_space=pltpu.VMEM)
    smem = pl.BlockSpec(memory_space=pltpu.SMEM)
    dma = pltpu.SemaphoreType.DMA
    return pl.pallas_call(
        functools.partial(fused_kernel, (n_side, n_z, n_sub, facet, SG)),
        out_shape=jax.ShapeDtypeStruct((n_sub, 2, urows, block), f32),
        in_specs=[pl.BlockSpec(memory_space=pl.ANY)] + [vmem] * 2 + [smem] * 6,
        out_specs=vmem,
        scratch_shapes=[
            pltpu.VMEM((facet, 2 * facet), b16),
            pltpu.VMEM((2, n_sub, SG, 2 * facet), b16),
            pltpu.VMEM((n_sub, facet, SG), f32),
            pltpu.VMEM((n_sub, facet, SG), f32),
            pltpu.VMEM((n_sub, facet, SG), f32),
            pltpu.VMEM((n_sub, 2 * facet, SG // 2), b16),
            pltpu.VMEM((n_sub, 2, SG, 2 * facet), b16),
            pltpu.VMEM((2, SG // ROWS, facet), f32),
            pltpu.VMEM((2, 2, ROWS, facet), f32),
            pltpu.VMEM((2, -(-2 * n_sub // 8) * 8, facet), f32),
            pltpu.VMEM((n_chunk, n_side, n_side, rows, block), f32),
            pltpu.VMEM((n_chunk, n_side - 1, n_side, rows, block), f32),
            pltpu.VMEM((n_chunk, n_side, rows, block), f32),
            pltpu.VMEM((n_chunk, n_side - 1, rows, block), f32),
            pltpu.VMEM((n_chunk, n_z, up, block), f32),
            pltpu.VMEM((n_chunk, n_z - 1, up, block), f32),
            pltpu.VMEM((n_z, n_side, n_side, up, block), f32),
            pltpu.VMEM((n_z - 1, n_side, n_side, up, block), f32),
            pltpu.VMEM((n_side, n_side, up, block), f32),
            pltpu.VMEM((n_side - 1, n_side, up, block), f32),
            pltpu.VMEM((n_side, up, block), f32),
            pltpu.VMEM((n_side - 1, up, block), f32),
            dma((2,)),
            dma((n_sub,)),
            dma((n_sub,)),
            dma((n_chunk, n_side - 1)),
            dma((n_chunk, n_side - 1)),
            dma((n_chunk, n_side - 1)),
            dma((n_chunk, n_side - 1)),
            dma((n_chunk, n_z - 1)),
            dma((n_chunk, n_z - 1)),
            dma((n_z - 1,)),
            dma((n_z - 1,)),
            dma((n_side - 1,)),
            dma((n_side - 1,)),
            dma((n_side - 1,)),
            dma((n_side - 1,)),
        ],
        compiler_params=pltpu.CompilerParams(
            collective_id=0, has_side_effects=True, vmem_limit_bytes=56 << 20
        ),
    )(image, window_rows.reshape(1, -1), window_cols.reshape(1, -1), *scalars)


def solution(mesh):
    n_side = mesh.shape["fcol"] // 2
    n_z = mesh.shape["frow"] // n_side
    tiled = (
        n_side >= 2
        and n_z >= 2
        and mesh.shape["fcol"] == 2 * n_side
        and mesh.shape["frow"] == n_z * n_side
        and SG % (2 * n_side * 128) == 0
        and SG % (n_side * n_z * ROWS * PARTS) == 0
    )

    def local(image, *rest):
        if tiled and image.shape[1] == image.shape[2] and image.shape[1] % 128 == 0:
            return fused_local(n_side, n_z, image, *rest)
        return general_local(image, *rest)

    placed = (P(None, "frow", "fcol"), P("frow"), P("fcol"), P(), P(), P(), P(), P(), P())
    return jax.shard_map(
        local, mesh=mesh, in_specs=placed, out_specs=P(None, None, "frow", "fcol"), check_vma=False
    )
```
